128 devices in a mesh: pair: 4 (over z_lo, core), shot: 32 (over x, y, z_hi).
Axes of the slice: x: 4, y: 4, z: 4 (z_hi: 2, z_lo: 2; z = z_hi * 2 + z_lo), core: 2. Of those that a mesh axis runs over, the one named last changes fastest.
Arguments:
- records: bfloat16 [8, 768, 768, 128], P('pair', 'shot'), may hold values from -6 to 6
- surface: float32 [32, 768], P('shot'), may hold values from 0.4 to 1.2
- mirror: int32 [8], replicated, may hold values from 0 to 7, as said below
Outputs:
- predicted: bfloat16 [8, 768, 768, 128], P('pair', 'shot')
The draws below stay inside these ranges and needn't reach their ends.
Inputs may be any that keep to these rules, and one draw needn't show every extreme that they name: mirror is an involution without fixed points: mirror[mirror[g]] = g and mirror[g] differs from g for every group.
All inputs are finite; a program needn't handle non-finite values.
Results may differ from the reference program's by a relative error of at most 0.0088.
Values may be sent and summed in bfloat16 or wider, within the bound.
No kernel may reach another device: no remote copies, remote signals or barrier semaphores. Data moves between devices by JAX's collectives and lax.ppermute only.
A program may use at most 128 MiB of HBM per device.

```python
import math
import jax
import jax.numpy as jnp
from jax import lax

SHOTS = 768
RECV = 768
TIME = 128
FREQS = 32
ORDERS = 2
GROUPS = 8


def draw_mirror(key, part):
    order = jax.random.permutation(key, GROUPS).astype(jnp.int32)
    evens = order[0::2]
    odds = order[1::2]
    paired = jnp.zeros((GROUPS,), jnp.int32).at[evens].set(odds).at[odds].set(evens)
    return paired


def block_scale(key, extent, split, low, high):
    def one(dim, parts):
        heights = jax.random.uniform(jax.random.fold_in(jax.random.fold_in(key, 6), dim), (parts,), jnp.float32, low / len(split), high / len(split))
        return jnp.repeat(jnp.exp(heights), extent[dim] // parts).reshape((-1,) + (1,) * (len(extent) - dim - 1))

    gain = one(*split[0])
    for cut in split[1:]:
        gain = gain * one(*cut)
    return gain


def noise(stream_key, shape, width, reach, cuts=(), held_as=jnp.bfloat16):
    entries = jax.random.normal(stream_key, shape, jnp.float32) * width
    if len(cuts) > 0:
        entries = block_scale(stream_key, shape, cuts, -0.22, 0.18) * entries
    return jnp.clip(entries, min=-reach, max=reach).astype(held_as)


def setup_inputs(seed: int = 0) -> dict:
    streams_of = jax.random.split(jax.random.key(seed), 4)
    records = noise(streams_of[0], (GROUPS, SHOTS, RECV, TIME), 1.0, 6.0, ((0, 4), (1, 32)))
    surface = jnp.clip(jnp.exp(math.log(1.2) - 1.0986123 * jax.random.uniform(streams_of[1], (FREQS, RECV), jnp.float32) ** block_scale(streams_of[1], (FREQS, RECV), ((0, 32),), -0.2, 0.2)), 0.4, 1.2)
    mirror = draw_mirror(jax.random.fold_in(streams_of[3], 71), 0)
    return dict(records=records, surface=surface, mirror=mirror)


def make_tables(freqs, time):
    product = jnp.arange(1, freqs + 1, dtype=jnp.int32)[:, None] * jnp.arange(time, dtype=jnp.int32)[None, :] % time
    phase = product.astype(jnp.float32) * (2.0 * math.pi / time)
    cosine = jnp.cos(phase)
    sine = jnp.sin(phase)
    forward = (jnp.stack([cosine, -sine], axis=1) * math.sqrt(2.0 / time)).astype(jnp.bfloat16)
    inverse = (jnp.stack([cosine, -sine], axis=1) / math.sqrt(freqs)).astype(jnp.bfloat16)
    return (forward, inverse)

def real_dot(left, right):
    return jnp.dot(left.astype(jnp.float32), right.astype(jnp.float32), precision=lax.Precision.HIGHEST)

def one_frequency(items):
    own_spec, mate_spec, column_scale = items
    left = (own_spec.astype(jnp.float32) * column_scale[None, None, :]).astype(jnp.bfloat16)
    total = jnp.zeros(own_spec.shape, jnp.float32)
    for order_index in range(ORDERS):
        real_part = real_dot(left[0], mate_spec[0]) - real_dot(left[1], mate_spec[1])
        imag_part = real_dot(left[0], mate_spec[1]) + real_dot(left[1], mate_spec[0])
        product = jnp.stack([real_part, imag_part], axis=0)
        total = total + product
        if order_index + 1 < ORDERS:
            left = (product * column_scale[None, None, :]).astype(jnp.bfloat16)
    return total.astype(jnp.bfloat16)

def reference(records, surface, mirror):
    forward, inverse = make_tables(FREQS, TIME)

    def group_spectra(group_records):
        return jnp.einsum('kct,srt->kcsr', forward.astype(jnp.float32), group_records.astype(jnp.float32), precision=lax.Precision.HIGHEST).astype(jnp.bfloat16)
    spectra = lax.map(group_spectra, records)
    mates = spectra[mirror]
    scale = -surface.astype(jnp.float32) / math.sqrt(2.0 * RECV)

    def one_group(items):
        own_group, mate_group = items
        totals = lax.map(one_frequency, (own_group, mate_group, scale))
        predicted = jnp.einsum('kcsr,kct->srt', totals.astype(jnp.float32), inverse.astype(jnp.float32), precision=lax.Precision.HIGHEST)
        return predicted.astype(jnp.bfloat16)
    return lax.map(one_group, (spectra, mates))
```

```python
import math

import jax
import jax.numpy as jnp
from jax import lax
from jax.experimental import pallas as pl
from jax.experimental.pallas import tpu as pltpu
from jax.sharding import Mesh
from jax.sharding import PartitionSpec as P

COLUMN = ("x", "y", "zh", "zl")
ROWS = 256


def make_tables(freqs, time):
    product = (
        jnp.arange(1, freqs + 1, dtype=jnp.int32)[:, None]
        * jnp.arange(time, dtype=jnp.int32)[None, :]
        % time
    )
    phase = product.astype(jnp.float32) * (2.0 * math.pi / time)
    cosine = jnp.cos(phase)
    sine = jnp.sin(phase)
    forward = (jnp.stack([cosine, -sine], axis=1) * math.sqrt(2.0 / time)).astype(jnp.bfloat16)
    inverse = (jnp.stack([cosine, -sine], axis=1) / math.sqrt(freqs)).astype(jnp.bfloat16)
    return (forward, inverse)


def deal(mirror):
    groups = mirror.shape[0]
    half = groups // 2
    index = jnp.arange(groups, dtype=jnp.int32)
    chip = index // half
    local = index % half
    within = (mirror // half) == chip
    crossing = groups - jnp.sum(within.astype(jnp.int32))
    low = jnp.minimum(index, mirror)
    color = jnp.where(
        crossing == groups,
        low >= half // 2,
        jnp.where(crossing == groups // 2, ~within, (local != 0) & (mirror % half != 0)),
    ).astype(jnp.int32)
    key = jnp.where(within, index, low)
    before = (
        (chip[:, None] == chip[None, :])
        & (color[:, None] == color[None, :])
        & (key[None, :] < key[:, None])
    )
    place = 2 * color + jnp.sum(before.astype(jnp.int32), axis=1)
    mixed = jnp.stack([crossing == groups, crossing >= groups // 2]).astype(jnp.int32)
    return place, mixed


def chain_body(scale_ref, own_ref, mate_ref, out_ref):
    scale = -scale_ref[...] / math.sqrt(2.0 * scale_ref.shape[-1])
    mate_re = mate_ref[0, 0]
    mate_im = mate_ref[0, 1]

    def dot(a, b):
        return jnp.dot(a, b, preferred_element_type=jnp.float32)

    def times(left_re, left_im):
        real = dot(left_re, mate_re) - dot(left_im, mate_im)
        imag = dot(left_re, mate_im) + dot(left_im, mate_re)
        return real, imag

    def scaled(part):
        return (part * scale).astype(jnp.bfloat16)

    real_1, imag_1 = times(
        scaled(own_ref[0, 0].astype(jnp.float32)), scaled(own_ref[0, 1].astype(jnp.float32))
    )
    real_2, imag_2 = times(scaled(real_1), scaled(imag_1))
    out_ref[0, 0] = (real_1 + real_2).astype(jnp.bfloat16)
    out_ref[0, 1] = (imag_1 + imag_2).astype(jnp.bfloat16)


def chain(pair, surface):
    members, parts, shots, recv = pair.shape
    rows = ROWS
    return pl.pallas_call(
        chain_body,
        grid=(members, shots // rows),
        in_specs=[
            pl.BlockSpec((1, recv), lambda j, m: (0, 0)),
            pl.BlockSpec((1, parts, rows, recv), lambda j, m: (j, 0, m, 0)),
            pl.BlockSpec((1, parts, shots, recv), lambda j, m: (1 - j, 0, 0, 0)),
        ],
        out_specs=pl.BlockSpec((1, parts, rows, recv), lambda j, m: (j, 0, m, 0)),
        out_shape=jax.ShapeDtypeStruct(pair.shape, jnp.bfloat16),
        compiler_params=pltpu.CompilerParams(vmem_limit_bytes=56 << 20),
    )(surface, pair, pair)


def pick(stack, where, axis):
    return [lax.dynamic_index_in_dim(stack, w, axis, keepdims=True) for w in where]


def other_core(part):
    return lax.ppermute(part, "core", [(0, 1), (1, 0)])


def local(records, surface, mirror):
    core = lax.axis_index("core")
    chip = lax.axis_index("zl")
    groups, shots, recv, time = records.shape
    freqs = lax.axis_size("x") * lax.axis_size("y") * lax.axis_size("zh")
    width = recv // 2
    forward, inverse = make_tables(freqs, time)
    place, mixed = deal(mirror)
    place = lax.dynamic_slice_in_dim(place, 2 * groups * chip, 2 * groups, 0)
    mixed = lax.dynamic_index_in_dim(mixed, chip, 0, keepdims=False)
    slots = jnp.arange(2 * groups, dtype=jnp.int32)
    order = jnp.sum(jnp.where(place[None, :] == slots[:, None], slots[None, :], 0), axis=1)

    def halves(whole, axis):
        kept = lax.dynamic_slice_in_dim(whole, core * width, width, axis)
        sent = lax.dynamic_slice_in_dim(whole, (1 - core) * width, width, axis)
        return kept, sent

    spectra = jnp.einsum(
        "kct,gsrt->kgcsr", forward, records, preferred_element_type=jnp.float32
    ).astype(jnp.bfloat16)
    kept, sent = halves(spectra, 4)
    both = jnp.concatenate([kept, other_core(sent)], axis=1)
    where = [
        jnp.where(order[i] // 2 == core, order[i] % 2, 2 + order[i] % 2) for i in range(2 * groups)
    ]
    chunks = jnp.concatenate(pick(both, where, 1), axis=1)
    chunks = chunks.reshape((2 * freqs, 2, 2, shots, width))
    chunks = lax.all_to_all(chunks, COLUMN, 0, 0, tiled=True)
    chunks = chunks.reshape((freqs, 4, 2, shots, width))

    def member(unit, j):
        return jnp.where(mixed == 1, 2 * j + unit, 2 * unit + j)

    kept = jnp.concatenate(pick(chunks, [member(core, j) for j in range(2)], 1), axis=1)
    sent = jnp.concatenate(pick(chunks, [member(1 - core, j) for j in range(2)], 1), axis=1)
    got = other_core(sent)
    first = jnp.where(core == 0, kept, got)
    second = jnp.where(core == 0, got, kept)
    pair = jnp.concatenate([first, second], axis=4)
    pair = pair.transpose(1, 2, 0, 3, 4).reshape((2, 2, freqs * shots, recv))

    total = chain(pair, surface)

    kept, sent = halves(total, 3)
    both = jnp.concatenate([kept, other_core(sent)], axis=0)
    both = both.reshape((4, 2, freqs, shots, width))
    where = []
    for i in range(4):
        unit = jnp.where(mixed == 1, i % 2, i // 2)
        j = jnp.where(mixed == 1, i // 2, i % 2)
        where.append(jnp.where(unit == core, j, 2 + j))
    chunks = jnp.concatenate(pick(both, where, 0), axis=0).transpose(2, 0, 1, 3, 4)
    chunks = chunks.reshape((2 * freqs, 2, 2, shots, width))
    chunks = lax.all_to_all(chunks, COLUMN, 0, 0, tiled=True)
    chunks = chunks.reshape((freqs, 4, 2, shots, width))
    kept = jnp.concatenate(pick(chunks, [place[2 * core + g] for g in range(groups)], 1), axis=1)
    sent = jnp.concatenate(
        pick(chunks, [place[2 * (1 - core) + g] for g in range(groups)], 1), axis=1
    )
    got = other_core(sent)
    first = jnp.where(core == 0, kept, got)
    second = jnp.where(core == 0, got, kept)
    total = jnp.concatenate([first, second], axis=4)
    return jnp.einsum(
        "kgcsr,kct->gsrt", total, inverse, preferred_element_type=jnp.float32
    ).astype(jnp.bfloat16)


def solution(mesh):
    devices = mesh.devices.reshape((2, 2, 4, 4, 2))
    whole = Mesh(devices, ("zl", "core", "x", "y", "zh"))
    pair, shot = ("zl", "core"), ("x", "y", "zh")
    return jax.shard_map(
        local,
        mesh=whole,
        in_specs=(P(pair, shot, None, None), P(shot, None), P()),
        out_specs=P(pair, shot, None, None),
        check_vma=False,
    )
```

```python
import math

import jax
import jax.numpy as jnp
from jax import lax
from jax.experimental import pallas as pl
from jax.experimental.pallas import tpu as pltpu
from jax.sharding import Mesh
from jax.sharding import PartitionSpec as P

COLUMN = ("x", "y", "zh", "zl")
ROWS = 384
SUBLANES = 8
GROUPS = 8
VMEM_LIMIT = 56 << 20


def make_tables(freqs, time):
    product = (
        jnp.arange(1, freqs + 1, dtype=jnp.int32)[:, None]
        * jnp.arange(time, dtype=jnp.int32)[None, :]
        % time
    )
    phase = product.astype(jnp.float32) * (2.0 * math.pi / time)
    cosine = jnp.cos(phase)
    sine = jnp.sin(phase)
    forward = (jnp.stack([cosine, -sine], axis=1) * math.sqrt(2.0 / time)).astype(jnp.bfloat16)
    inverse = (jnp.stack([cosine, -sine], axis=1) / math.sqrt(freqs)).astype(jnp.bfloat16)
    return (forward, inverse)


OWN_SLOT = 0
OTHER_SLOT = 2
OWN_MEMBER = 4
OTHER_MEMBER = 6
HALF = 8
OTHER_HALF = 9
FLAT = 10
ENTRIES = 12


def deal_body(mirror_ref, here_ref, table_ref):
    half = GROUPS // 2
    chip, core = here_ref[0], here_ref[1]
    mirror = [mirror_ref[g] for g in range(GROUPS)]
    zero, one = jnp.int32(0), jnp.int32(1)

    def flag(condition):
        return jnp.where(condition, one, zero)

    upper = [flag(m >= half) for m in mirror]
    within = [upper[g] if g >= half else 1 - upper[g] for g in range(GROUPS)]
    crossing = GROUPS - sum(within[1:], within[0])
    low = [jnp.minimum(m, g) for g, m in enumerate(mirror)]
    color, key = [], []
    for g in range(GROUPS):
        with_first = flag(mirror[g] - half * upper[g] == 0) if g % half else one
        color.append(
            jnp.where(
                crossing == GROUPS,
                flag(low[g] >= half // 2),
                jnp.where(crossing == half, 1 - within[g], 1 - with_first),
            )
        )
        key.append(jnp.where(within[g] == 1, g, low[g]))
    place = []
    for g in range(GROUPS):
        rank = zero
        for other in range(g // half * half, g // half * half + half):
            if other != g:
                rank = rank + flag(color[g] == color[other]) * flag(key[other] < key[g])
        place.append(2 * color[g] + rank)
    mine = [jnp.where(chip == 0, place[g], place[half + g]) for g in range(half)]
    for g in range(2):
        table_ref[OWN_SLOT + g] = jnp.where(core == 0, mine[g], mine[2 + g])
        table_ref[OTHER_SLOT + g] = jnp.where(core == 0, mine[2 + g], mine[g])
    mixed = jnp.where(chip == 0, flag(crossing == GROUPS), flag(crossing >= half))
    for j in range(2):
        table_ref[OWN_MEMBER + j] = jnp.where(mixed == 1, 2 * j + core, 2 * core + j)
        table_ref[OTHER_MEMBER + j] = jnp.where(mixed == 1, 2 * j + 1 - core, 2 * (1 - core) + j)
    table_ref[HALF] = core
    table_ref[OTHER_HALF] = 1 - core
    table_ref[FLAT] = zero
    table_ref[FLAT + 1] = one


def deal(mirror, here):
    smem = pl.BlockSpec(memory_space=pltpu.SMEM)
    return pl.pallas_call(
        deal_body,
        in_specs=[smem, smem],
        out_specs=smem,
        out_shape=jax.ShapeDtypeStruct((ENTRIES,), jnp.int32),
        name="deal",
    )(mirror, here)


def params():
    return pltpu.CompilerParams(vmem_limit_bytes=VMEM_LIMIT)


def two_shots(taps_ref):
    taps = taps_ref[...]
    blank = jnp.zeros_like(taps)
    return jnp.concatenate(
        [jnp.concatenate([taps, blank], axis=1), jnp.concatenate([blank, taps], axis=1)], axis=0
    )


def forward_transform(table, forward, records, half, slots, count):
    groups, shots, recv, time = records.shape
    parts = forward.shape[0]
    width = recv // 2
    tiles = shots // SUBLANES

    def body(table_ref, forward_ref, records_ref, out_ref, held, spectra, in_sems, out_sems):
        start = pl.multiple_of(table_ref[half] * width, width)
        ins, outs = [], []
        for i in range(groups * tiles):
            g, s = divmod(i, tiles)
            source = records_ref.at[g, pl.ds(s * SUBLANES, SUBLANES), pl.ds(start, width)]
            ins.append(pltpu.make_async_copy(source, held.at[i], in_sems.at[i]))
        for copy in ins:
            copy.start()
        two = two_shots(forward_ref)
        for i in range(groups * tiles):
            g, s = divmod(i, tiles)
            ins[i].wait()
            found = []
            for q in range(0, SUBLANES, 2):
                both = jnp.concatenate([held[i, q], held[i, q + 1]], axis=1)
                found.append(
                    lax.dot_general(
                        two, both, (((1,), (1,)), ((), ())), preferred_element_type=jnp.float32
                    )
                )
            found = jnp.concatenate(found, axis=0).reshape((SUBLANES, parts, width))
            found = jnp.transpose(found, (1, 0, 2)).reshape((parts // 2, 2, SUBLANES, width))
            spectra[g, :, :, s * SUBLANES : (s + 1) * SUBLANES, :] = found.astype(jnp.bfloat16)
            if s == tiles - 1:
                target = out_ref.at[:, table_ref[slots + g]]
                outs.append(pltpu.make_async_copy(spectra.at[g], target, out_sems.at[g]))
                outs[-1].start()
        for copy in outs:
            copy.wait()

    return pl.pallas_call(
        body,
        in_specs=[
            pl.BlockSpec(memory_space=pltpu.SMEM),
            pl.BlockSpec(memory_space=pltpu.VMEM),
            pl.BlockSpec(memory_space=pl.ANY),
        ],
        out_specs=pl.BlockSpec(memory_space=pl.ANY),
        out_shape=jax.ShapeDtypeStruct((parts // 2, count, 2, shots, width), jnp.bfloat16),
        scratch_shapes=[
            pltpu.VMEM((groups * tiles, SUBLANES, width, time), jnp.bfloat16),
            pltpu.VMEM((groups, parts // 2, 2, shots, width), jnp.bfloat16),
            pltpu.SemaphoreType.DMA((groups * tiles,)),
            pltpu.SemaphoreType.DMA((groups,)),
        ],
        compiler_params=params(),
        name="forward",
    )(table, forward, records)


def copy_slots(pairs, sems):
    copies = [pltpu.make_async_copy(a, b, sems.at[i]) for i, (a, b) in enumerate(pairs)]
    for copy in copies:
        copy.start()
    for copy in copies:
        copy.wait()


def gather(table, whole, slots):
    blocks, _, parts, shots, width = whole.shape

    def body(table_ref, whole_ref, part_ref, sems):
        copy_slots(
            [(whole_ref.at[:, table_ref[slots + j]], part_ref.at[:, j]) for j in range(2)], sems
        )

    return pl.pallas_call(
        body,
        in_specs=[pl.BlockSpec(memory_space=pltpu.SMEM), pl.BlockSpec(memory_space=pl.ANY)],
        out_specs=pl.BlockSpec(memory_space=pltpu.VMEM),
        out_shape=jax.ShapeDtypeStruct((blocks, 2, parts, shots, width), jnp.bfloat16),
        scratch_shapes=[pltpu.SemaphoreType.DMA((2,))],
        compiler_params=params(),
        name="gather",
    )(table, whole)


def scatter(table, part, whole, slots):
    def body(table_ref, part_ref, whole_ref, out_ref, sems):
        copy_slots(
            [(part_ref.at[:, j], out_ref.at[:, table_ref[slots + j]]) for j in range(2)], sems
        )

    return pl.pallas_call(
        body,
        in_specs=[
            pl.BlockSpec(memory_space=pltpu.SMEM),
            pl.BlockSpec(memory_space=pltpu.VMEM),
            pl.BlockSpec(memory_space=pl.ANY),
        ],
        out_specs=pl.BlockSpec(memory_space=pl.ANY),
        out_shape=jax.ShapeDtypeStruct(whole.shape, jnp.bfloat16),
        scratch_shapes=[pltpu.SemaphoreType.DMA((2,))],
        input_output_aliases={2: 0},
        compiler_params=params(),
        name="scatter",
    )(table, part, whole)


def chain_body(
    table_ref, scale_ref, kept_0_ref, kept_1_ref, got_ref, own_ref, other_ref, spectra_ref
):
    member, tile = pl.program_id(0), pl.program_id(1)
    blocks, _, _, shots, width = got_ref.shape
    size = blocks * shots
    core = table_ref[HALF]

    @pl.when((member == 0) & (tile == 0))
    def _():
        for value in range(2):

            @pl.when(core == value)
            def _():
                for j, kept_ref in enumerate((kept_0_ref, kept_1_ref)):
                    for c in range(2):
                        kept = kept_ref[:, 0, c].reshape((size, width))
                        got = got_ref[:, j, c].reshape((size, width))
                        spectra_ref[j, c, :, value * width : (value + 1) * width] = kept
                        spectra_ref[j, c, :, (1 - value) * width : (2 - value) * width] = got

    rows = own_ref.shape[0] * shots
    scale = -scale_ref[...] / math.sqrt(2.0 * scale_ref.shape[-1])
    mate_re = spectra_ref[1 - member, 0]
    mate_im = spectra_ref[1 - member, 1]

    def dot(a, b):
        return jnp.dot(a, b, preferred_element_type=jnp.float32)

    def times(left_re, left_im):
        real = dot(left_re, mate_re) - dot(left_im, mate_im)
        imag = dot(left_re, mate_im) + dot(left_im, mate_re)
        return real, imag

    def scaled(part):
        return (part * scale).astype(jnp.bfloat16)

    window = pl.ds(pl.multiple_of(tile * rows, rows), rows)
    real_1, imag_1 = times(
        scaled(spectra_ref[member, 0, window, :].astype(jnp.float32)),
        scaled(spectra_ref[member, 1, window, :].astype(jnp.float32)),
    )
    real_2, imag_2 = times(scaled(real_1), scaled(imag_1))
    for c, total in enumerate((real_1 + real_2, imag_1 + imag_2)):
        total = total.astype(jnp.bfloat16)
        low = total[:, :width].reshape((rows // shots, shots, width))
        high = total[:, width:].reshape((rows // shots, shots, width))

        @pl.when(core == 0)
        def _():
            own_ref[:, 0, c] = low
            other_ref[:, 0, c] = high

        @pl.when(core == 1)
        def _():
            own_ref[:, 0, c] = high
            other_ref[:, 0, c] = low


def chain(table, surface, kept, got):
    blocks, count, parts, shots, width = kept.shape
    tile = ROWS // shots
    tiles = blocks // tile
    whole = (blocks, 1, parts, shots, width)
    part = (tile, 1, parts, shots, width)
    return pl.pallas_call(
        chain_body,
        grid_spec=pltpu.PrefetchScalarGridSpec(
            num_scalar_prefetch=1,
            grid=(2, tiles),
            in_specs=[
                pl.BlockSpec((1, 2 * width), lambda j, m, t: (0, 0)),
                pl.BlockSpec(whole, lambda j, m, t: (0, t[OWN_MEMBER], 0, 0, 0)),
                pl.BlockSpec(whole, lambda j, m, t: (0, t[OWN_MEMBER + 1], 0, 0, 0)),
                pl.BlockSpec(memory_space=pltpu.VMEM),
            ],
            out_specs=[
                pl.BlockSpec(part, lambda j, m, t: (m, t[OWN_MEMBER + j], 0, 0, 0)),
                pl.BlockSpec(part, lambda j, m, t: (m, j, 0, 0, 0)),
            ],
            scratch_shapes=[pltpu.VMEM((2, parts, blocks * shots, 2 * width), jnp.bfloat16)],
        ),
        out_shape=[
            jax.ShapeDtypeStruct(kept.shape, jnp.bfloat16),
            jax.ShapeDtypeStruct(got.shape, jnp.bfloat16),
        ],
        compiler_params=params(),
        name="chain",
    )(table, surface, kept, kept, got)


def inverse_transform(table, inverse, total, half, slots, whole=None):
    freqs, count, parts, shots, width = total.shape
    rows, time = inverse.shape
    tiles = shots // SUBLANES
    groups = 2
    pieces = 2
    local_input = count == groups

    def body(table_ref, inverse_ref, total_ref, *refs):
        out_ref, held, predicted, in_sems, out_sems = refs[-5:]
        start = pl.multiple_of(table_ref[half] * width, width)
        ins, outs = [], []
        if not local_input:
            for g in range(groups):
                for p in range(pieces):
                    some = pl.ds(p * freqs // pieces, freqs // pieces)
                    source = total_ref.at[some, table_ref[slots + g]]
                    ins.append(
                        pltpu.make_async_copy(source, held.at[g, some], in_sems.at[g, p])
                    )
            for copy in ins:
                copy.start()
        two = two_shots(inverse_ref)
        for g in range(groups):
            if not local_input:
                for copy in ins[g * pieces : (g + 1) * pieces]:
                    copy.wait()
            for s in range(tiles):
                window = slice(s * SUBLANES, (s + 1) * SUBLANES)
                block = total_ref[:, g, :, window, :] if local_input else held[g, :, :, window, :]
                block = block.astype(jnp.float32).reshape((rows, SUBLANES, width))
                block = jnp.transpose(block, (1, 0, 2)).astype(jnp.bfloat16)
                i = g * tiles + s
                for q in range(0, SUBLANES, 2):
                    both = jnp.concatenate([block[q], block[q + 1]], axis=0)
                    traces = lax.dot_general(
                        both, two, (((0,), (0,)), ((), ())), preferred_element_type=jnp.float32
                    ).astype(jnp.bfloat16)
                    predicted[i, q] = traces[:, :time]
                    predicted[i, q + 1] = traces[:, time:]
                target = out_ref.at[g, pl.ds(s * SUBLANES, SUBLANES), pl.ds(start, width)]
                outs.append(pltpu.make_async_copy(predicted.at[i], target, out_sems.at[i]))
                outs[-1].start()
        for copy in outs:
            copy.wait()

    specs = [
        pl.BlockSpec(memory_space=pltpu.SMEM),
        pl.BlockSpec(memory_space=pltpu.VMEM),
        pl.BlockSpec(memory_space=pltpu.VMEM if local_input else pl.ANY),
    ]
    operands = [table, inverse, total]
    aliases = {}
    if whole is not None:
        specs.append(pl.BlockSpec(memory_space=pl.ANY))
        operands.append(whole)
        aliases = {3: 0}
    return pl.pallas_call(
        body,
        in_specs=specs,
        out_specs=pl.BlockSpec(memory_space=pl.ANY),
        out_shape=jax.ShapeDtypeStruct((groups, shots, 2 * width, time), jnp.bfloat16),
        scratch_shapes=[
            pltpu.VMEM((groups, freqs, parts, shots, width), jnp.bfloat16),
            pltpu.VMEM((groups * tiles, SUBLANES, width, time), jnp.bfloat16),
            pltpu.SemaphoreType.DMA((groups, pieces)),
            pltpu.SemaphoreType.DMA((groups * tiles,)),
        ],
        input_output_aliases=aliases,
        compiler_params=params(),
        name="inverse",
    )(*operands)


def other_core(part):
    part = lax.ppermute(part, "core", [(0, 1), (1, 0)])
    return pltpu.with_memory_space_constraint(part, pltpu.VMEM)


def exchange(chunks):
    blocks, count, parts, shots, width = chunks.shape
    chunks = chunks.reshape((2 * blocks, count // 2, parts, shots, width))
    chunks = lax.all_to_all(chunks, COLUMN, 0, 0, tiled=True)
    return chunks.reshape((blocks, count, parts, shots, width))


def local(records, surface, mirror):
    freqs = lax.axis_size("x") * lax.axis_size("y") * lax.axis_size("zh")
    time = records.shape[-1]
    forward, inverse = make_tables(freqs, time)
    forward = forward.reshape((2 * freqs, time))
    inverse = inverse.reshape((2 * freqs, time))
    here = jnp.stack([lax.axis_index("zl"), lax.axis_index("core")]).astype(jnp.int32)
    table = deal(mirror, here)

    sent = forward_transform(table, forward, records, OTHER_HALF, FLAT, 2)
    chunks = forward_transform(table, forward, records, HALF, OWN_SLOT, 4)
    chunks = scatter(table, other_core(sent), chunks, OTHER_SLOT)
    chunks = exchange(chunks)
    got = other_core(gather(table, chunks, OTHER_MEMBER))
    own, other = chain(table, surface, chunks, got)
    chunks = scatter(table, other_core(other), own, OTHER_MEMBER)
    chunks = exchange(chunks)
    got = other_core(gather(table, chunks, OTHER_SLOT))
    predicted = inverse_transform(table, inverse, chunks, HALF, OWN_SLOT)
    return inverse_transform(table, inverse, got, OTHER_HALF, FLAT, predicted)


def solution(mesh):
    devices = mesh.devices.reshape((2, 2, 4, 4, 2))
    whole = Mesh(devices, ("zl", "core", "x", "y", "zh"))
    pair, shot = ("zl", "core"), ("x", "y", "zh")
    return jax.shard_map(
        local,
        mesh=whole,
        in_specs=(P(pair, shot, None, None), P(shot, None), P()),
        out_specs=P(pair, shot, None, None),
        check_vma=False,
    )
```

```python
import math

import jax
import jax.numpy as jnp
import numpy as np
from jax import lax
from jax.experimental import pallas as pl
from jax.experimental.pallas import tpu as pltpu
from jax.sharding import Mesh
from jax.sharding import PartitionSpec as P

COLUMN = ("x", "y", "zh", "zl")
ROWS = 384
SUBLANES = 8
GROUPS = 8


def make_tables(freqs, time):
    product = np.arange(1, freqs + 1)[:, None] * np.arange(time)[None, :] % time
    phase = product * (2.0 * math.pi / time)
    parts = np.stack([np.cos(phase), -np.sin(phase)], axis=1).reshape((2 * freqs, time))
    forward = (parts * math.sqrt(2.0 / time)).astype(np.float32)
    inverse = (parts / math.sqrt(freqs)).astype(np.float32)
    return (forward.astype(jnp.bfloat16), inverse.astype(jnp.bfloat16))


OWN_SLOT = 0
OTHER_SLOT = 2
OWN_MEMBER = 4
OTHER_MEMBER = 6
ENTRIES = 8


def deal(mirror_ref, table_ref):
    half = GROUPS // 2
    chip, core = lax.axis_index("zl"), lax.axis_index("core")
    mirror = [mirror_ref[g] for g in range(GROUPS)]
    zero, one = jnp.int32(0), jnp.int32(1)

    def flag(condition):
        return jnp.where(condition, one, zero)

    upper = [flag(m >= half) for m in mirror]
    within = [upper[g] if g >= half else 1 - upper[g] for g in range(GROUPS)]
    crossing = GROUPS - sum(within[1:], within[0])
    low = [jnp.minimum(m, g) for g, m in enumerate(mirror)]
    color, key = [], []
    for g in range(GROUPS):
        with_first = flag(mirror[g] - half * upper[g] == 0) if g % half else one
        color.append(
            jnp.where(
                crossing == GROUPS,
                flag(low[g] >= half // 2),
                jnp.where(crossing == half, 1 - within[g], 1 - with_first),
            )
        )
        key.append(jnp.where(within[g] == 1, g, low[g]))
    place = []
    for g in range(GROUPS):
        rank = zero
        for other in range(g // half * half, g // half * half + half):
            if other != g:
                rank = rank + flag(color[g] == color[other]) * flag(key[other] < key[g])
        place.append(2 * color[g] + rank)
    mine = [jnp.where(chip == 0, place[g], place[half + g]) for g in range(half)]
    for g in range(2):
        table_ref[OWN_SLOT + g] = jnp.where(core == 0, mine[g], mine[2 + g])
        table_ref[OTHER_SLOT + g] = jnp.where(core == 0, mine[2 + g], mine[g])
    mixed = jnp.where(chip == 0, flag(crossing == GROUPS), flag(crossing >= half))
    for j in range(2):
        table_ref[OWN_MEMBER + j] = jnp.where(mixed == 1, 2 * j + core, 2 * core + j)
        table_ref[OTHER_MEMBER + j] = jnp.where(mixed == 1, 2 * j + 1 - core, 2 * (1 - core) + j)


def params(limit):
    return pltpu.CompilerParams(vmem_limit_bytes=limit << 20)


SMEM = pl.BlockSpec(memory_space=pltpu.SMEM)
VMEM = pl.BlockSpec(memory_space=pltpu.VMEM)
ANY = pl.BlockSpec(memory_space=pl.ANY)
HBM = pl.BlockSpec(memory_space=pltpu.HBM)


def copy_all(pairs, sems):
    copies = [pltpu.make_async_copy(a, b, sems.at[i]) for i, (a, b) in enumerate(pairs)]
    for copy in copies:
        copy.start()
    for copy in copies:
        copy.wait()


def gather(table, whole, slots):
    blocks, _, parts, shots, width = whole.shape

    def body(table_ref, whole_ref, part_ref, sems):
        copy_all(
            [(whole_ref.at[:, table_ref[slots + j]], part_ref.at[:, j]) for j in range(2)], sems
        )

    return pl.pallas_call(
        body,
        in_specs=[SMEM, VMEM],
        out_specs=VMEM,
        out_shape=on_chip((blocks, 2, parts, shots, width)),
        scratch_shapes=[pltpu.SemaphoreType.DMA((2,))],
        compiler_params=params(8),
        name="gather",
    )(table, whole)


def scatter(table, part, whole, slots):
    def body(table_ref, part_ref, whole_ref, out_ref, sems):
        copy_all(
            [(part_ref.at[:, j], out_ref.at[:, table_ref[slots + j]]) for j in range(2)], sems
        )

    return pl.pallas_call(
        body,
        in_specs=[SMEM, VMEM, VMEM],
        out_specs=VMEM,
        out_shape=on_chip(whole.shape),
        scratch_shapes=[pltpu.SemaphoreType.DMA((2,))],
        input_output_aliases={2: 0},
        compiler_params=params(8),
        name="scatter",
    )(table, part, whole)


def on_chip(shape):
    return pltpu.VMEM(shape, jnp.bfloat16)


def two_shots(taps_ref):
    taps = taps_ref[...]
    blank = jnp.zeros_like(taps)
    return jnp.concatenate(
        [jnp.concatenate([taps, blank], axis=1), jnp.concatenate([blank, taps], axis=1)], axis=0
    )


def forward_transform(forward, records, mirror=None):
    groups, shots, recv, time = records.shape
    parts = forward.shape[0]
    width = recv // 2
    tiles = shots // SUBLANES
    count = groups if mirror is None else 2 * groups
    shape = (parts // 2, count, 2, shots, width)

    def body(forward_ref, records_ref, *refs):
        held, in_sems = refs[-2:]
        core = lax.axis_index("core")
        half = 1 - core if mirror is None else core
        start = pl.multiple_of(half * width, width)
        copies = []
        for i in range(groups * tiles):
            g, s = divmod(i, tiles)
            source = records_ref.at[g, pl.ds(s * SUBLANES, SUBLANES), pl.ds(start, width)]
            copies.append(pltpu.make_async_copy(source, held.at[i], in_sems.at[i]))
        for copy in copies:
            copy.start()
        two = two_shots(forward_ref)
        if mirror is None:
            (out_ref,) = refs[:-2]
            slots = range(groups)
        else:
            mirror_ref, out_ref, table_ref = refs[:-2]
            deal(mirror_ref, table_ref)
            slots = [table_ref[OWN_SLOT + g] for g in range(groups)]
        for i in range(groups * tiles):
            g, s = divmod(i, tiles)
            copies[i].wait()
            found = []
            for q in range(0, SUBLANES, 2):
                both = jnp.concatenate([held[i, q], held[i, q + 1]], axis=1)
                found.append(
                    lax.dot_general(
                        two, both, (((1,), (1,)), ((), ())), preferred_element_type=jnp.float32
                    )
                )
            found = jnp.concatenate(found, axis=0).reshape((SUBLANES, parts, width))
            found = jnp.transpose(found, (1, 0, 2)).reshape((parts // 2, 2, SUBLANES, width))
            window = slice(s * SUBLANES, (s + 1) * SUBLANES)
            out_ref[:, slots[g], :, window, :] = found.astype(jnp.bfloat16)

    scratch = [
        pltpu.VMEM((groups * tiles, SUBLANES, width, time), jnp.bfloat16),
        pltpu.SemaphoreType.DMA((groups * tiles,)),
    ]
    if mirror is None:
        return pl.pallas_call(
            body,
            in_specs=[VMEM, HBM],
            out_specs=VMEM,
            out_shape=on_chip(shape),
            scratch_shapes=scratch,
            compiler_params=params(16),
            name="forward",
        )(forward, records)
    return pl.pallas_call(
        body,
        in_specs=[VMEM, HBM, SMEM],
        out_specs=[VMEM, SMEM],
        out_shape=[on_chip(shape), jax.ShapeDtypeStruct((ENTRIES,), jnp.int32)],
        scratch_shapes=scratch,
        compiler_params=params(16),
        name="forward",
    )(forward, records, mirror)


def chain(table, surface, kept, got):
    blocks, _, parts, shots, width = kept.shape
    size = blocks * shots
    step = ROWS // shots

    def body(table_ref, scale_ref, kept_ref, got_ref, own_ref, other_ref, spectra_ref):
        core = lax.axis_index("core")
        slots = [table_ref[OWN_MEMBER + j] for j in range(2)]
        for value in range(2):

            @pl.when(core == value)
            def _():
                here = slice(value * width, (value + 1) * width)
                there = slice((1 - value) * width, (2 - value) * width)
                for j in range(2):
                    for c in range(2):
                        spectra_ref[j, c, :, here] = kept_ref[:, slots[j], c].reshape((size, width))
                        spectra_ref[j, c, :, there] = got_ref[:, j, c].reshape((size, width))

        scale = -scale_ref[...] / math.sqrt(2.0 * scale_ref.shape[-1])
        for j in range(2):
            both = spectra_ref[j, 0].astype(jnp.float32) + spectra_ref[j, 1].astype(jnp.float32)
            spectra_ref[j, 2] = both.astype(jnp.bfloat16)

        def dot(a, b):
            return jnp.dot(a, b, preferred_element_type=jnp.float32)

        def scaled(part):
            return (part * scale).astype(jnp.bfloat16)

        def times(left_re, left_im, mate):
            both = (left_re.astype(jnp.float32) + left_im.astype(jnp.float32)).astype(jnp.bfloat16)
            first = dot(left_re, spectra_ref[mate, 0])
            second = dot(left_im, spectra_ref[mate, 1])
            third = dot(both, spectra_ref[mate, 2])
            return first - second, third - first - second

        for j in range(2):
            for m in range(blocks // step):
                window = pl.ds(m * ROWS, ROWS)
                real_1, imag_1 = times(
                    scaled(spectra_ref[j, 0, window, :].astype(jnp.float32)),
                    scaled(spectra_ref[j, 1, window, :].astype(jnp.float32)),
                    1 - j,
                )
                real_2, imag_2 = times(scaled(real_1), scaled(imag_1), 1 - j)
                for c, total in enumerate((real_1 + real_2, imag_1 + imag_2)):
                    total = total.astype(jnp.bfloat16)
                    low = total[:, :width].reshape((step, shots, width))
                    high = total[:, width:].reshape((step, shots, width))

                    @pl.when(core == 0)
                    def _():
                        own_ref[pl.ds(m * step, step), slots[j], c] = low
                        other_ref[pl.ds(m * step, step), j, c] = high

                    @pl.when(core == 1)
                    def _():
                        own_ref[pl.ds(m * step, step), slots[j], c] = high
                        other_ref[pl.ds(m * step, step), j, c] = low

    return pl.pallas_call(
        body,
        in_specs=[SMEM, VMEM, VMEM, VMEM],
        out_specs=[VMEM, VMEM],
        out_shape=[on_chip(kept.shape), on_chip(got.shape)],
        scratch_shapes=[pltpu.VMEM((2, 3, size, 2 * width), jnp.bfloat16)],
        compiler_params=params(30),
        name="chain",
    )(table, surface, kept, got)


def inverse_transform(table, inverse, total, slots=None, whole=None):
    _, _, parts, shots, width = total.shape
    rows, time = inverse.shape
    tiles = shots // SUBLANES
    groups = 2

    def body(table_ref, inverse_ref, total_ref, *refs):
        out_ref, predicted, out_sems = refs[-3:]
        core = lax.axis_index("core")
        half = core if whole is None else 1 - core
        start = pl.multiple_of(half * width, width)
        two = two_shots(inverse_ref)
        copies = []
        for i in range(groups * tiles):
            g, s = divmod(i, tiles)
            slot = g if slots is None else table_ref[slots + g]
            block = total_ref[:, slot, :, s * SUBLANES : (s + 1) * SUBLANES, :]
            block = block.astype(jnp.float32).reshape((rows, SUBLANES, width))
            block = jnp.transpose(block, (1, 0, 2)).astype(jnp.bfloat16)
            for q in range(0, SUBLANES, 2):
                both = jnp.concatenate([block[q], block[q + 1]], axis=0)
                traces = lax.dot_general(
                    both, two, (((0,), (0,)), ((), ())), preferred_element_type=jnp.float32
                ).astype(jnp.bfloat16)
                predicted[i, q] = traces[:, :time]
                predicted[i, q + 1] = traces[:, time:]
            target = out_ref.at[g, pl.ds(s * SUBLANES, SUBLANES), pl.ds(start, width)]
            copies.append(pltpu.make_async_copy(predicted.at[i], target, out_sems.at[i]))
            copies[-1].start()
        for copy in copies:
            copy.wait()

    specs = [SMEM, VMEM, VMEM]
    operands = [table, inverse, total]
    aliases = {}
    if whole is not None:
        specs.append(ANY)
        operands.append(whole)
        aliases = {3: 0}
    return pl.pallas_call(
        body,
        in_specs=specs,
        out_specs=ANY,
        out_shape=jax.ShapeDtypeStruct((groups, shots, 2 * width, time), jnp.bfloat16),
        scratch_shapes=[
            pltpu.VMEM((groups * tiles, SUBLANES, width, time), jnp.bfloat16),
            pltpu.SemaphoreType.DMA((groups * tiles,)),
        ],
        input_output_aliases=aliases,
        compiler_params=params(16),
        name="inverse",
    )(*operands)


def stay(part):
    return pltpu.with_memory_space_constraint(part, pltpu.VMEM)


def other_core(part):
    return stay(lax.ppermute(part, "core", [(0, 1), (1, 0)]))


def exchange(chunks):
    blocks, count, parts, shots, width = chunks.shape
    chunks = chunks.reshape((2 * blocks, count // 2, parts, shots, width))
    chunks = lax.all_to_all(chunks, COLUMN, 0, 0, tiled=True)
    return stay(chunks.reshape((blocks, count, parts, shots, width)))


def local(records, surface, mirror):
    freqs = lax.axis_size("x") * lax.axis_size("y") * lax.axis_size("zh")
    forward, inverse = make_tables(freqs, records.shape[-1])

    sent = forward_transform(forward, records)
    chunks, table = forward_transform(forward, records, mirror)
    chunks = scatter(table, other_core(sent), chunks, OTHER_SLOT)
    chunks = exchange(chunks)
    got = other_core(gather(table, chunks, OTHER_MEMBER))
    own, other = chain(table, surface, chunks, got)
    chunks = scatter(table, other_core(other), own, OTHER_MEMBER)
    chunks = exchange(chunks)
    got = other_core(gather(table, chunks, OTHER_SLOT))
    predicted = inverse_transform(table, inverse, chunks, OWN_SLOT)
    return inverse_transform(table, inverse, got, None, predicted)


def solution(mesh):
    devices = mesh.devices.reshape((2, 2, 4, 4, 2))
    whole = Mesh(devices, ("zl", "core", "x", "y", "zh"))
    pair, shot = ("zl", "core"), ("x", "y", "zh")
    return jax.shard_map(
        local,
        mesh=whole,
        in_specs=(P(pair, shot, None, None), P(shot, None), P()),
        out_specs=P(pair, shot, None, None),
        check_vma=False,
    )
```

```python
import math

import jax
import jax.numpy as jnp
import numpy as np
from jax import lax
from jax.experimental import pallas as pl
from jax.experimental.pallas import tpu as pltpu
from jax.sharding import Mesh
from jax.sharding import PartitionSpec as P

COLUMN = ("x", "y", "zh", "zl")
ROWS = 384
SUBLANES = 8
GROUPS = 8


def make_tables(freqs, time):
    product = np.arange(1, freqs + 1)[:, None] * np.arange(time)[None, :] % time
    phase = product * (2.0 * math.pi / time)
    parts = np.stack([np.cos(phase), -np.sin(phase)], axis=1).reshape((2 * freqs, time))
    forward = (parts * math.sqrt(2.0 / time)).astype(np.float32)
    inverse = (parts / math.sqrt(freqs)).astype(np.float32)
    return (forward.astype(jnp.bfloat16), inverse.astype(jnp.bfloat16))


OWN_SLOT = 0
OTHER_SLOT = 2
OWN_MEMBER = 4
OTHER_MEMBER = 6
ENTRIES = 8


def deal(mirror_ref, table_ref):
    half = GROUPS // 2
    chip, core = lax.axis_index("zl"), lax.axis_index("core")
    mirror = [mirror_ref[g] for g in range(GROUPS)]
    zero, one = jnp.int32(0), jnp.int32(1)

    def flag(condition):
        return jnp.where(condition, one, zero)

    upper = [flag(m >= half) for m in mirror]
    within = [upper[g] if g >= half else 1 - upper[g] for g in range(GROUPS)]
    crossing = GROUPS - sum(within[1:], within[0])
    low = [jnp.minimum(m, g) for g, m in enumerate(mirror)]
    color, key = [], []
    for g in range(GROUPS):
        with_first = flag(mirror[g] - half * upper[g] == 0) if g % half else one
        color.append(
            jnp.where(
                crossing == GROUPS,
                flag(low[g] >= half // 2),
                jnp.where(crossing == half, 1 - within[g], 1 - with_first),
            )
        )
        key.append(jnp.where(within[g] == 1, g, low[g]))
    place = []
    for g in range(GROUPS):
        rank = zero
        for other in range(g // half * half, g // half * half + half):
            if other != g:
                rank = rank + flag(color[g] == color[other]) * flag(key[other] < key[g])
        place.append(2 * color[g] + rank)
    mine = [jnp.where(chip == 0, place[g], place[half + g]) for g in range(half)]
    for g in range(2):
        table_ref[OWN_SLOT + g] = jnp.where(core == 0, mine[g], mine[2 + g])
        table_ref[OTHER_SLOT + g] = jnp.where(core == 0, mine[2 + g], mine[g])
    mixed = jnp.where(chip == 0, flag(crossing == GROUPS), flag(crossing >= half))
    for j in range(2):
        table_ref[OWN_MEMBER + j] = jnp.where(mixed == 1, 2 * j + core, 2 * core + j)
        table_ref[OTHER_MEMBER + j] = jnp.where(mixed == 1, 2 * j + 1 - core, 2 * (1 - core) + j)


def params(limit):
    return pltpu.CompilerParams(vmem_limit_bytes=limit << 20)


SMEM = pl.BlockSpec(memory_space=pltpu.SMEM)
VMEM = pl.BlockSpec(memory_space=pltpu.VMEM)
ANY = pl.BlockSpec(memory_space=pl.ANY)
HBM = pl.BlockSpec(memory_space=pltpu.HBM)


def copy_all(pairs, sems):
    copies = [pltpu.make_async_copy(a, b, sems.at[i]) for i, (a, b) in enumerate(pairs)]
    for copy in copies:
        copy.start()
    for copy in copies:
        copy.wait()


def gather(table, whole, slots):
    blocks, _, parts, shots, width = whole.shape

    def body(table_ref, whole_ref, part_ref, sems):
        copy_all(
            [(whole_ref.at[:, table_ref[slots + j]], part_ref.at[:, j]) for j in range(2)], sems
        )

    return pl.pallas_call(
        body,
        in_specs=[SMEM, VMEM],
        out_specs=VMEM,
        out_shape=on_chip((blocks, 2, parts, shots, width)),
        scratch_shapes=[pltpu.SemaphoreType.DMA((2,))],
        compiler_params=params(8),
        name="gather",
    )(table, whole)


def scatter(table, parts, whole, slots):
    places = [(p, j) for p, part in enumerate(parts) for j in range(part.shape[1])]

    def body(table_ref, *refs):
        out_ref, sems = refs[-2:]
        copy_all(
            [
                (refs[p].at[:, j], out_ref.at[:, table_ref[slots + i]])
                for i, (p, j) in enumerate(places)
            ],
            sems,
        )

    return pl.pallas_call(
        body,
        in_specs=[SMEM] + [VMEM] * (len(parts) + 1),
        out_specs=VMEM,
        out_shape=on_chip(whole.shape),
        scratch_shapes=[pltpu.SemaphoreType.DMA((len(places),))],
        input_output_aliases={len(parts) + 1: 0},
        compiler_params=params(8),
        name="scatter",
    )(table, *parts, whole)


def on_chip(shape):
    return pltpu.VMEM(shape, jnp.bfloat16)


def two_shots(taps_ref):
    taps = taps_ref[...]
    blank = jnp.zeros_like(taps)
    return jnp.concatenate(
        [jnp.concatenate([taps, blank], axis=1), jnp.concatenate([blank, taps], axis=1)], axis=0
    )


def forward_transform(forward, records, mirror=None):
    groups, shots, recv, time = records.shape
    parts = forward.shape[0]
    width = recv // 2
    tiles = shots // SUBLANES
    count = groups if mirror is None else 2 * groups
    shape = (parts // 2, count, 2, shots, width)

    def body(forward_ref, records_ref, *refs):
        held, taps, in_sems = refs[-3:]
        core = lax.axis_index("core")
        half = 1 - core if mirror is None else core
        start = pl.multiple_of(half * width, width)
        copies = []
        table_copy = pltpu.make_async_copy(forward_ref, taps, in_sems.at[groups * tiles])
        table_copy.start()
        for i in range(groups * tiles):
            g, s = divmod(i, tiles)
            source = records_ref.at[g, pl.ds(s * SUBLANES, SUBLANES), pl.ds(start, width)]
            copies.append(pltpu.make_async_copy(source, held.at[i], in_sems.at[i]))
        for copy in copies:
            copy.start()
        table_copy.wait()
        two = two_shots(taps)
        if mirror is None:
            (out_ref,) = refs[:-3]
            slots = range(groups)
        else:
            mirror_ref, out_ref, table_ref = refs[:-3]
            deal(mirror_ref, table_ref)
            slots = [table_ref[OWN_SLOT + g] for g in range(groups)]
        for i in range(groups * tiles):
            g, s = divmod(i, tiles)
            copies[i].wait()
            found = []
            for q in range(0, SUBLANES, 2):
                both = jnp.concatenate([held[i, q], held[i, q + 1]], axis=1)
                found.append(
                    lax.dot_general(
                        two, both, (((1,), (1,)), ((), ())), preferred_element_type=jnp.float32
                    )
                )
            found = jnp.concatenate(found, axis=0).reshape((SUBLANES, parts, width))
            found = jnp.transpose(found, (1, 0, 2)).reshape((parts // 2, 2, SUBLANES, width))
            window = slice(s * SUBLANES, (s + 1) * SUBLANES)
            out_ref[:, slots[g], :, window, :] = found.astype(jnp.bfloat16)

    scratch = [
        pltpu.VMEM((groups * tiles, SUBLANES, width, time), jnp.bfloat16),
        pltpu.VMEM((parts, time), jnp.bfloat16),
        pltpu.SemaphoreType.DMA((groups * tiles + 1,)),
    ]
    if mirror is None:
        return pl.pallas_call(
            body,
            in_specs=[HBM, HBM],
            out_specs=VMEM,
            out_shape=on_chip(shape),
            scratch_shapes=scratch,
            compiler_params=params(16),
            name="forward",
        )(forward, records)
    return pl.pallas_call(
        body,
        in_specs=[HBM, HBM, SMEM],
        out_specs=[VMEM, SMEM],
        out_shape=[on_chip(shape), jax.ShapeDtypeStruct((ENTRIES,), jnp.int32)],
        scratch_shapes=scratch,
        compiler_params=params(16),
        name="forward",
    )(forward, records, mirror)


def multiply(j, slot, scale_ref, spectra_ref, own_ref, other_ref):
    size, recv = spectra_ref.shape[-2:]
    blocks, _, _, shots, width = other_ref.shape
    step = ROWS // shots
    core = lax.axis_index("core")
    scale = -scale_ref[...] / math.sqrt(2.0 * recv)

    def dot(a, b):
        return jnp.dot(a, b, preferred_element_type=jnp.float32)

    def scaled(part):
        return (part * scale).astype(jnp.bfloat16)

    def times(left_re, left_im):
        both = (left_re.astype(jnp.float32) + left_im.astype(jnp.float32)).astype(jnp.bfloat16)
        first = dot(left_re, spectra_ref[1 - j, 0])
        second = dot(left_im, spectra_ref[1 - j, 1])
        third = dot(both, spectra_ref[1 - j, 2])
        return first - second, third - first - second

    for m in range(blocks // step):
        window = pl.ds(m * ROWS, ROWS)
        real_1, imag_1 = times(
            scaled(spectra_ref[j, 0, window, :].astype(jnp.float32)),
            scaled(spectra_ref[j, 1, window, :].astype(jnp.float32)),
        )
        real_2, imag_2 = times(scaled(real_1), scaled(imag_1))
        for c, total in enumerate((real_1 + real_2, imag_1 + imag_2)):
            total = total.astype(jnp.bfloat16)
            low = total[:, :width].reshape((step, shots, width))
            high = total[:, width:].reshape((step, shots, width))
            own_ref[pl.ds(m * step, step), slot, c] = jnp.where(core == 0, low, high)
            other_ref[pl.ds(m * step, step), 0, c] = jnp.where(core == 0, high, low)


def chain_first(table, surface, kept, got):
    blocks, _, parts, shots, width = kept.shape
    size = blocks * shots

    def body(table_ref, scale_ref, kept_ref, got_ref, own_ref, other_ref, spectra_ref):
        core = lax.axis_index("core")
        slots = [table_ref[OWN_MEMBER + j] for j in range(2)]
        for value in range(2):

            @pl.when(core == value)
            def _():
                here = slice(value * width, (value + 1) * width)
                there = slice((1 - value) * width, (2 - value) * width)
                for j in range(2):
                    for c in range(2):
                        spectra_ref[j, c, :, here] = kept_ref[:, slots[j], c].reshape((size, width))
                        spectra_ref[j, c, :, there] = got_ref[:, j, c].reshape((size, width))

        for j in range(2):
            both = spectra_ref[j, 0].astype(jnp.float32) + spectra_ref[j, 1].astype(jnp.float32)
            spectra_ref[j, 2] = both.astype(jnp.bfloat16)
        multiply(0, slots[0], scale_ref, spectra_ref, own_ref, other_ref)

    return pl.pallas_call(
        body,
        in_specs=[SMEM, VMEM, VMEM, VMEM],
        out_specs=[VMEM, VMEM, VMEM],
        out_shape=[
            on_chip(kept.shape),
            on_chip((blocks, 1, parts, shots, width)),
            on_chip((2, 3, size, 2 * width)),
        ],
        compiler_params=params(20),
        name="chain",
    )(table, surface, kept, got)


def chain_second(table, surface, spectra, own, other):
    def body(table_ref, scale_ref, spectra_ref, first_ref, own_ref, other_ref):
        slot = table_ref[OWN_MEMBER + 1]
        multiply(1, slot, scale_ref, spectra_ref, own_ref, other_ref)

    return pl.pallas_call(
        body,
        in_specs=[SMEM, VMEM, VMEM, VMEM],
        out_specs=[VMEM, VMEM],
        out_shape=[on_chip(own.shape), on_chip(other.shape)],
        input_output_aliases={3: 0},
        compiler_params=params(20),
        name="chain",
    )(table, surface, spectra, own)


def inverse_transform(table, inverse, total, slots=None, whole=None):
    _, _, parts, shots, width = total.shape
    rows, time = inverse.shape
    tiles = shots // SUBLANES
    groups = 2

    def body(table_ref, inverse_ref, total_ref, *refs):
        out_ref, predicted, out_sems = refs[-3:]
        core = lax.axis_index("core")
        half = core if whole is None else 1 - core
        start = pl.multiple_of(half * width, width)
        two = two_shots(inverse_ref)
        copies = []
        for i in range(groups * tiles):
            g, s = divmod(i, tiles)
            slot = g if slots is None else table_ref[slots + g]
            block = total_ref[:, slot, :, s * SUBLANES : (s + 1) * SUBLANES, :]
            block = block.astype(jnp.float32).reshape((rows, SUBLANES, width))
            block = jnp.transpose(block, (1, 0, 2)).astype(jnp.bfloat16)
            for q in range(0, SUBLANES, 2):
                both = jnp.concatenate([block[q], block[q + 1]], axis=0)
                traces = lax.dot_general(
                    both, two, (((0,), (0,)), ((), ())), preferred_element_type=jnp.float32
                ).astype(jnp.bfloat16)
                predicted[i, q] = traces[:, :time]
                predicted[i, q + 1] = traces[:, time:]
            target = out_ref.at[g, pl.ds(s * SUBLANES, SUBLANES), pl.ds(start, width)]
            copies.append(pltpu.make_async_copy(predicted.at[i], target, out_sems.at[i]))
            copies[-1].start()
        for copy in copies:
            copy.wait()

    specs = [SMEM, VMEM, VMEM]
    operands = [table, inverse, total]
    aliases = {}
    if whole is not None:
        specs.append(ANY)
        operands.append(whole)
        aliases = {3: 0}
    return pl.pallas_call(
        body,
        in_specs=specs,
        out_specs=ANY,
        out_shape=jax.ShapeDtypeStruct((groups, shots, 2 * width, time), jnp.bfloat16),
        scratch_shapes=[
            pltpu.VMEM((groups * tiles, SUBLANES, width, time), jnp.bfloat16),
            pltpu.SemaphoreType.DMA((groups * tiles,)),
        ],
        input_output_aliases=aliases,
        compiler_params=params(16),
        name="inverse",
    )(*operands)


def stay(part):
    return pltpu.with_memory_space_constraint(part, pltpu.VMEM)


def other_core(part):
    return stay(lax.ppermute(part, "core", [(0, 1), (1, 0)]))


def exchange(chunks):
    blocks, count, parts, shots, width = chunks.shape
    chunks = chunks.reshape((2 * blocks, count // 2, parts, shots, width))
    chunks = lax.all_to_all(chunks, COLUMN, 0, 0, tiled=True)
    return stay(chunks.reshape((blocks, count, parts, shots, width)))


def local(records, surface, mirror):
    freqs = lax.axis_size("x") * lax.axis_size("y") * lax.axis_size("zh")
    forward, inverse = make_tables(freqs, records.shape[-1])
    forward = pltpu.with_memory_space_constraint(forward, pltpu.HBM)
    records = pltpu.with_memory_space_constraint(records, pltpu.HBM)
    sent = forward_transform(forward, records)
    chunks, table = forward_transform(forward, records, mirror)
    chunks = scatter(table, [other_core(sent)], chunks, OTHER_SLOT)
    chunks = exchange(chunks)
    got = other_core(gather(table, chunks, OTHER_MEMBER))
    own, first, spectra = chain_first(table, surface, chunks, got)
    first_got = other_core(first)
    own, second = chain_second(table, surface, spectra, own, first)
    chunks = scatter(table, [first_got, other_core(second)], own, OTHER_MEMBER)
    chunks = exchange(chunks)
    got = other_core(gather(table, chunks, OTHER_SLOT))
    predicted = inverse_transform(table, inverse, chunks, OWN_SLOT)
    return inverse_transform(table, inverse, got, None, predicted)


def solution(mesh):
    devices = mesh.devices.reshape((2, 2, 4, 4, 2))
    whole = Mesh(devices, ("zl", "core", "x", "y", "zh"))
    pair, shot = ("zl", "core"), ("x", "y", "zh")
    return jax.shard_map(
        local,
        mesh=whole,
        in_specs=(P(pair, shot, None, None), P(shot, None), P()),
        out_specs=P(pair, shot, None, None),
        check_vma=False,
    )
```

```python
import math

import jax
import jax.numpy as jnp
import numpy as np
from jax import lax
from jax.experimental import pallas as pl
from jax.experimental.pallas import tpu as pltpu
from jax.sharding import Mesh
from jax.sharding import PartitionSpec as P

COLUMN = ("x", "y", "zh", "zl")
ROWS = 384
SUBLANES = 8
AHEAD = 2
GROUPS = 8


def make_tables(freqs, time):
    product = np.arange(1, freqs + 1)[:, None] * np.arange(time)[None, :] % time
    phase = product * (2.0 * math.pi / time)
    parts = np.stack([np.cos(phase), -np.sin(phase)], axis=1).reshape((2 * freqs, time))
    forward = (parts * math.sqrt(2.0 / time)).astype(np.float32)
    inverse = (parts / math.sqrt(freqs)).astype(np.float32)
    return (forward.astype(jnp.bfloat16), inverse.astype(jnp.bfloat16))


OWN_SLOT = 0
OTHER_SLOT = 2
OWN_MEMBER = 4
OTHER_MEMBER = 6
ENTRIES = 8


def deal(mirror_ref, table_ref):
    half = GROUPS // 2
    chip, core = lax.axis_index("zl"), lax.axis_index("core")
    mirror = [mirror_ref[g] for g in range(GROUPS)]
    zero, one = jnp.int32(0), jnp.int32(1)

    def flag(condition):
        return jnp.where(condition, one, zero)

    upper = [flag(m >= half) for m in mirror]
    within = [upper[g] if g >= half else 1 - upper[g] for g in range(GROUPS)]
    crossing = GROUPS - sum(within[1:], within[0])
    low = [jnp.minimum(m, g) for g, m in enumerate(mirror)]
    color, key = [], []
    for g in range(GROUPS):
        with_first = flag(mirror[g] - half * upper[g] == 0) if g % half else one
        color.append(
            jnp.where(
                crossing == GROUPS,
                flag(low[g] >= half // 2),
                jnp.where(crossing == half, 1 - within[g], 1 - with_first),
            )
        )
        key.append(jnp.where(within[g] == 1, g, low[g]))
    place = []
    for g in range(GROUPS):
        rank = zero
        for other in range(g // half * half, g // half * half + half):
            if other != g:
                rank = rank + flag(color[g] == color[other]) * flag(key[other] < key[g])
        place.append(2 * color[g] + rank)
    mine = [jnp.where(chip == 0, place[g], place[half + g]) for g in range(half)]
    for g in range(2):
        table_ref[OWN_SLOT + g] = jnp.where(core == 0, mine[g], mine[2 + g])
        table_ref[OTHER_SLOT + g] = jnp.where(core == 0, mine[2 + g], mine[g])
    mixed = jnp.where(chip == 0, flag(crossing == GROUPS), flag(crossing >= half))
    for j in range(2):
        table_ref[OWN_MEMBER + j] = jnp.where(mixed == 1, 2 * j + core, 2 * core + j)
        table_ref[OTHER_MEMBER + j] = jnp.where(mixed == 1, 2 * j + 1 - core, 2 * (1 - core) + j)


def params(limit):
    return pltpu.CompilerParams(vmem_limit_bytes=limit << 20)


SMEM = pl.BlockSpec(memory_space=pltpu.SMEM)
VMEM = pl.BlockSpec(memory_space=pltpu.VMEM)
ANY = pl.BlockSpec(memory_space=pl.ANY)
HBM = pl.BlockSpec(memory_space=pltpu.HBM)


def copy_all(pairs, sems):
    copies = [pltpu.make_async_copy(a, b, sems.at[i]) for i, (a, b) in enumerate(pairs)]
    for copy in copies:
        copy.start()
    for copy in copies:
        copy.wait()


def gather(table, whole, entries):
    blocks, _, parts, shots, width = whole.shape
    count = len(entries)

    def body(table_ref, whole_ref, part_ref, sems):
        copy_all(
            [(whole_ref.at[:, table_ref[e]], part_ref.at[:, j]) for j, e in enumerate(entries)],
            sems,
        )

    return pl.pallas_call(
        body,
        in_specs=[SMEM, VMEM],
        out_specs=VMEM,
        out_shape=on_chip((blocks, count, parts, shots, width)),
        scratch_shapes=[pltpu.SemaphoreType.DMA((count,))],
        compiler_params=params(8),
        name="gather",
    )(table, whole)


def scatter(table, parts, whole, slots):
    places = [(p, j) for p, part in enumerate(parts) for j in range(part.shape[1])]

    def body(table_ref, *refs):
        out_ref, sems = refs[-2:]
        copy_all(
            [
                (refs[p].at[:, j], out_ref.at[:, table_ref[slots + i]])
                for i, (p, j) in enumerate(places)
            ],
            sems,
        )

    return pl.pallas_call(
        body,
        in_specs=[SMEM] + [VMEM] * (len(parts) + 1),
        out_specs=VMEM,
        out_shape=on_chip(whole.shape),
        scratch_shapes=[pltpu.SemaphoreType.DMA((len(places),))],
        input_output_aliases={len(parts) + 1: 0},
        compiler_params=params(8),
        name="scatter",
    )(table, *parts, whole)


def on_chip(shape):
    return pltpu.VMEM(shape, jnp.bfloat16)


def two_shots(taps_ref):
    taps = taps_ref[...]
    blank = jnp.zeros_like(taps)
    return jnp.concatenate(
        [jnp.concatenate([taps, blank], axis=1), jnp.concatenate([blank, taps], axis=1)], axis=0
    )


def forward_transform(forward, records, mirror=None, ahead=None):
    groups, shots, recv, time = records.shape
    parts = forward.shape[0]
    width = recv // 2
    tiles = shots // SUBLANES
    count = groups if mirror is None else 2 * groups
    shape = (parts // 2, count, 2, shots, width)
    early = (AHEAD, SUBLANES, width, time)

    def body(forward_ref, records_ref, *refs):
        held, taps, in_sems = refs[-3:]
        core = lax.axis_index("core")

        def fetch(i, half, target, sem):
            g, s = divmod(i, tiles)
            start = pl.multiple_of(half * width, width)
            source = records_ref.at[g, pl.ds(s * SUBLANES, SUBLANES), pl.ds(start, width)]
            copy = pltpu.make_async_copy(source, target, in_sems.at[sem])
            copy.start()
            return copy

        table_copy = pltpu.make_async_copy(forward_ref, taps, in_sems.at[groups * tiles])
        table_copy.start()
        waiting = {}
        if mirror is None:
            out_ref, ahead_ref = refs[:-3]
            for i in range(groups * tiles):
                waiting[i] = fetch(i, 1 - core, held.at[i], i)
            late = [
                fetch(i, core, ahead_ref.at[i], groups * tiles + 1 + i) for i in range(AHEAD)
            ]
            slots = range(groups)
        else:
            mirror_ref, ahead_ref, out_ref, table_ref = refs[:-3]
            for i in range(AHEAD, groups * tiles):
                waiting[i] = fetch(i, core, held.at[i], i)
            late = []
            deal(mirror_ref, table_ref)
            slots = [table_ref[OWN_SLOT + g] for g in range(groups)]
        table_copy.wait()
        two = two_shots(taps)
        for i in range(groups * tiles):
            g, s = divmod(i, tiles)
            if i in waiting:
                waiting[i].wait()
            block_ref = held if i in waiting else ahead_ref
            found = []
            for q in range(0, SUBLANES, 2):
                both = jnp.concatenate([block_ref[i, q], block_ref[i, q + 1]], axis=1)
                found.append(
                    lax.dot_general(
                        two, both, (((1,), (1,)), ((), ())), preferred_element_type=jnp.float32
                    )
                )
            found = jnp.concatenate(found, axis=0).reshape((SUBLANES, parts, width))
            found = jnp.transpose(found, (1, 0, 2)).reshape((parts // 2, 2, SUBLANES, width))
            window = slice(s * SUBLANES, (s + 1) * SUBLANES)
            out_ref[:, slots[g], :, window, :] = found.astype(jnp.bfloat16)
        for copy in late:
            copy.wait()

    scratch = [
        pltpu.VMEM((groups * tiles, SUBLANES, width, time), jnp.bfloat16),
        pltpu.VMEM((parts, time), jnp.bfloat16),
        pltpu.SemaphoreType.DMA((groups * tiles + 1 + AHEAD,)),
    ]
    if mirror is None:
        return pl.pallas_call(
            body,
            in_specs=[HBM, HBM],
            out_specs=[VMEM, VMEM],
            out_shape=[on_chip(shape), on_chip(early)],
            scratch_shapes=scratch,
            compiler_params=params(16),
            name="forward",
        )(forward, records)
    return pl.pallas_call(
        body,
        in_specs=[HBM, HBM, SMEM, VMEM],
        out_specs=[VMEM, SMEM],
        out_shape=[on_chip(shape), jax.ShapeDtypeStruct((ENTRIES,), jnp.int32)],
        scratch_shapes=scratch,
        compiler_params=params(16),
        name="forward",
    )(forward, records, mirror, ahead)


def multiply(j, slot, scale_ref, spectra_ref, own_ref, other_ref):
    size, recv = spectra_ref.shape[-2:]
    blocks, _, _, shots, width = other_ref.shape
    step = ROWS // shots
    core = lax.axis_index("core")
    scale = -scale_ref[...] / math.sqrt(2.0 * recv)

    def dot(a, b):
        return jnp.dot(a, b, preferred_element_type=jnp.float32)

    def scaled(part):
        return (part * scale).astype(jnp.bfloat16)

    def times(left_re, left_im):
        both = left_re + left_im
        first = dot(left_re, spectra_ref[1 - j, 0])
        second = dot(left_im, spectra_ref[1 - j, 1])
        third = dot(both, spectra_ref[1 - j, 2])
        return first - second, third - first - second

    for m in range(blocks // step):
        window = pl.ds(m * ROWS, ROWS)
        real_1, imag_1 = times(
            scaled(spectra_ref[j, 0, window, :].astype(jnp.float32)),
            scaled(spectra_ref[j, 1, window, :].astype(jnp.float32)),
        )
        real_2, imag_2 = times(scaled(real_1), scaled(imag_1))
        for c, total in enumerate((real_1 + real_2, imag_1 + imag_2)):
            total = total.astype(jnp.bfloat16)
            low = total[:, :width].reshape((step, shots, width))
            high = total[:, width:].reshape((step, shots, width))
            own_ref[pl.ds(m * step, step), slot, c] = jnp.where(core == 0, low, high)
            other_ref[pl.ds(m * step, step), j, c] = jnp.where(core == 0, high, low)


def chain(table, surface, kept, got):
    blocks, _, parts, shots, width = kept.shape
    size = blocks * shots

    def body(table_ref, scale_ref, kept_ref, got_ref, own_ref, other_ref, spectra_ref):
        core = lax.axis_index("core")
        slots = [table_ref[OWN_MEMBER + j] for j in range(2)]
        for value in range(2):

            @pl.when(core == value)
            def _():
                here = slice(value * width, (value + 1) * width)
                there = slice((1 - value) * width, (2 - value) * width)
                for j in range(2):
                    for c in range(2):
                        spectra_ref[j, c, :, here] = kept_ref[:, slots[j], c].reshape((size, width))
                        spectra_ref[j, c, :, there] = got_ref[:, j, c].reshape((size, width))

        for j in range(2):
            spectra_ref[j, 2] = spectra_ref[j, 0] + spectra_ref[j, 1]
        for j in range(2):
            multiply(j, slots[j], scale_ref, spectra_ref, own_ref, other_ref)

    return pl.pallas_call(
        body,
        in_specs=[SMEM, VMEM, VMEM, VMEM],
        out_specs=[VMEM, VMEM],
        out_shape=[on_chip(kept.shape), on_chip(got.shape)],
        scratch_shapes=[pltpu.VMEM((2, 3, size, 2 * width), jnp.bfloat16)],
        compiler_params=params(30),
        name="chain",
    )(table, surface, kept, got)


def inverse_transform(table, inverse, total, groups, whole=None):
    _, _, parts, shots, width = total.shape
    rows, time = inverse.shape
    tiles = shots // SUBLANES
    count = len(groups)

    def body(table_ref, inverse_ref, total_ref, *refs):
        out_ref, predicted, out_sems = refs[-3:]
        core = lax.axis_index("core")
        half = core if whole is None else 1 - core
        start = pl.multiple_of(half * width, width)
        two = two_shots(inverse_ref)
        copies = []
        for i in range(count * tiles):
            n, s = divmod(i, tiles)
            g = groups[n]
            slot = table_ref[OWN_SLOT + g] if whole is None else n
            block = total_ref[:, slot, :, s * SUBLANES : (s + 1) * SUBLANES, :]
            block = block.astype(jnp.float32).reshape((rows, SUBLANES, width))
            block = jnp.transpose(block, (1, 0, 2)).astype(jnp.bfloat16)
            for q in range(0, SUBLANES, 2):
                both = jnp.concatenate([block[q], block[q + 1]], axis=0)
                traces = lax.dot_general(
                    both, two, (((0,), (0,)), ((), ())), preferred_element_type=jnp.float32
                ).astype(jnp.bfloat16)
                predicted[i, q] = traces[:, :time]
                predicted[i, q + 1] = traces[:, time:]
            target = out_ref.at[g, pl.ds(s * SUBLANES, SUBLANES), pl.ds(start, width)]
            copies.append(pltpu.make_async_copy(predicted.at[i], target, out_sems.at[i]))
            copies[-1].start()
        for copy in copies:
            copy.wait()

    specs = [SMEM, VMEM, VMEM]
    operands = [table, inverse, total]
    aliases = {}
    if whole is not None:
        specs.append(ANY)
        operands.append(whole)
        aliases = {3: 0}
    return pl.pallas_call(
        body,
        in_specs=specs,
        out_specs=ANY,
        out_shape=jax.ShapeDtypeStruct((2, shots, 2 * width, time), jnp.bfloat16),
        scratch_shapes=[
            pltpu.VMEM((count * tiles, SUBLANES, width, time), jnp.bfloat16),
            pltpu.SemaphoreType.DMA((count * tiles,)),
        ],
        input_output_aliases=aliases,
        compiler_params=params(16),
        name="inverse",
    )(*operands)


def stay(part):
    return pltpu.with_memory_space_constraint(part, pltpu.VMEM)


def other_core(part):
    return stay(lax.ppermute(part, "core", [(0, 1), (1, 0)]))


def exchange(chunks):
    blocks, count, parts, shots, width = chunks.shape
    chunks = chunks.reshape((2 * blocks, count // 2, parts, shots, width))
    chunks = lax.all_to_all(chunks, COLUMN, 0, 0, tiled=True)
    return stay(chunks.reshape((blocks, count, parts, shots, width)))


def local(records, surface, mirror):
    freqs = lax.axis_size("x") * lax.axis_size("y") * lax.axis_size("zh")
    forward, inverse = make_tables(freqs, records.shape[-1])
    forward = pltpu.with_memory_space_constraint(forward, pltpu.HBM)
    records = pltpu.with_memory_space_constraint(records, pltpu.HBM)
    sent, ahead = forward_transform(forward, records)
    chunks, table = forward_transform(forward, records, mirror, ahead)
    chunks = scatter(table, [other_core(sent)], chunks, OTHER_SLOT)
    chunks = exchange(chunks)
    got = other_core(gather(table, chunks, [OTHER_MEMBER, OTHER_MEMBER + 1]))
    own, other = chain(table, surface, chunks, got)
    chunks = scatter(table, [other_core(other)], own, OTHER_MEMBER)
    chunks = exchange(chunks)
    got = [other_core(gather(table, chunks, [OTHER_SLOT + g])) for g in range(2)]
    predicted = inverse_transform(table, inverse, chunks, [0, 1])
    for g in range(2):
        predicted = inverse_transform(table, inverse, got[g], [g], predicted)
    return predicted


def solution(mesh):
    devices = mesh.devices.reshape((2, 2, 4, 4, 2))
    whole = Mesh(devices, ("zl", "core", "x", "y", "zh"))
    pair, shot = ("zl", "core"), ("x", "y", "zh")
    return jax.shard_map(
        local,
        mesh=whole,
        in_specs=(P(pair, shot, None, None), P(shot, None), P()),
        out_specs=P(pair, shot, None, None),
        check_vma=False,
    )
```

```python
import math

import jax
import jax.numpy as jnp
import numpy as np
from jax import lax
from jax.experimental import pallas as pl
from jax.experimental.pallas import tpu as pltpu
from jax.sharding import Mesh
from jax.sharding import PartitionSpec as P

COLUMN = ("x", "y", "zh", "zl")
ROWS = 384
SUBLANES = 8
AHEAD = 2
GROUPS = 8


def make_tables(freqs, time):
    product = np.arange(1, freqs + 1)[:, None] * np.arange(time)[None, :] % time
    phase = product * (2.0 * math.pi / time)
    parts = np.stack([np.cos(phase), -np.sin(phase)], axis=1).reshape((2 * freqs, time))
    forward = (parts * math.sqrt(2.0 / time)).astype(np.float32)
    inverse = (parts / math.sqrt(freqs)).astype(np.float32)
    return (forward.astype(jnp.bfloat16), inverse.astype(jnp.bfloat16))


OWN_SLOT = 0
OTHER_SLOT = 2
OWN_MEMBER = 4
OTHER_MEMBER = 6
ENTRIES = 8


def deal(mirror_ref, table_ref):
    half = GROUPS // 2
    chip, core = lax.axis_index("zl"), lax.axis_index("core")
    mirror = [mirror_ref[g] for g in range(GROUPS)]
    zero, one = jnp.int32(0), jnp.int32(1)

    def flag(condition):
        return jnp.where(condition, one, zero)

    upper = [flag(m >= half) for m in mirror]
    within = [upper[g] if g >= half else 1 - upper[g] for g in range(GROUPS)]
    crossing = GROUPS - sum(within[1:], within[0])
    low = [jnp.minimum(m, g) for g, m in enumerate(mirror)]
    color, key = [], []
    for g in range(GROUPS):
        with_first = flag(mirror[g] - half * upper[g] == 0) if g % half else one
        color.append(
            jnp.where(
                crossing == GROUPS,
                flag(low[g] >= half // 2),
                jnp.where(crossing == half, 1 - within[g], 1 - with_first),
            )
        )
        key.append(jnp.where(within[g] == 1, g, low[g]))
    place = []
    for g in range(GROUPS):
        rank = zero
        for other in range(g // half * half, g // half * half + half):
            if other != g:
                rank = rank + flag(color[g] == color[other]) * flag(key[other] < key[g])
        place.append(2 * color[g] + rank)
    mine = [jnp.where(chip == 0, place[g], place[half + g]) for g in range(half)]
    for g in range(2):
        table_ref[OWN_SLOT + g] = jnp.where(core == 0, mine[g], mine[2 + g])
        table_ref[OTHER_SLOT + g] = jnp.where(core == 0, mine[2 + g], mine[g])
    mixed = jnp.where(chip == 0, flag(crossing == GROUPS), flag(crossing >= half))
    for j in range(2):
        table_ref[OWN_MEMBER + j] = jnp.where(mixed == 1, 2 * j + core, 2 * core + j)
        table_ref[OTHER_MEMBER + j] = jnp.where(mixed == 1, 2 * j + 1 - core, 2 * (1 - core) + j)


def params(limit):
    return pltpu.CompilerParams(vmem_limit_bytes=limit << 20)


SMEM = pl.BlockSpec(memory_space=pltpu.SMEM)
VMEM = pl.BlockSpec(memory_space=pltpu.VMEM)
ANY = pl.BlockSpec(memory_space=pl.ANY)
HBM = pl.BlockSpec(memory_space=pltpu.HBM)


def copy_all(pairs, sems):
    copies = [pltpu.make_async_copy(a, b, sems.at[i]) for i, (a, b) in enumerate(pairs)]
    for copy in copies:
        copy.start()
    for copy in copies:
        copy.wait()


def gather(table, whole, entries):
    blocks, _, parts, shots, width = whole.shape
    count = len(entries)

    def body(table_ref, whole_ref, part_ref, sems):
        copy_all(
            [(whole_ref.at[:, table_ref[e]], part_ref.at[:, j]) for j, e in enumerate(entries)],
            sems,
        )

    return pl.pallas_call(
        body,
        in_specs=[SMEM, VMEM],
        out_specs=VMEM,
        out_shape=on_chip((blocks, count, parts, shots, width)),
        scratch_shapes=[pltpu.SemaphoreType.DMA((count,))],
        compiler_params=params(8),
        name="gather",
    )(table, whole)


def scatter(table, parts, whole, slots):
    places = [(p, j) for p, part in enumerate(parts) for j in range(part.shape[1])]

    def body(table_ref, *refs):
        out_ref, sems = refs[-2:]
        copy_all(
            [
                (refs[p].at[:, j], out_ref.at[:, table_ref[slots + i]])
                for i, (p, j) in enumerate(places)
            ],
            sems,
        )

    return pl.pallas_call(
        body,
        in_specs=[SMEM] + [VMEM] * (len(parts) + 1),
        out_specs=VMEM,
        out_shape=on_chip(whole.shape),
        scratch_shapes=[pltpu.SemaphoreType.DMA((len(places),))],
        input_output_aliases={len(parts) + 1: 0},
        compiler_params=params(8),
        name="scatter",
    )(table, *parts, whole)


def on_chip(shape):
    return pltpu.VMEM(shape, jnp.bfloat16)


def two_shots(taps_ref):
    taps = taps_ref[...]
    blank = jnp.zeros_like(taps)
    return jnp.concatenate(
        [jnp.concatenate([taps, blank], axis=1), jnp.concatenate([blank, taps], axis=1)], axis=0
    )


def forward_transform(forward, records, mirror=None, ahead=None):
    groups, shots, recv, time = records.shape
    parts = forward.shape[0]
    width = recv // 2
    tiles = shots // SUBLANES
    count = groups if mirror is None else 2 * groups
    shape = (parts // 2, count, 2, shots, width)
    early = (AHEAD, SUBLANES, width, time)

    def body(forward_ref, records_ref, *refs):
        held, taps, in_sems = refs[-3:]
        core = lax.axis_index("core")

        def fetch(i, half, target, sem):
            g, s = divmod(i, tiles)
            start = pl.multiple_of(half * width, width)
            source = records_ref.at[g, pl.ds(s * SUBLANES, SUBLANES), pl.ds(start, width)]
            copy = pltpu.make_async_copy(source, target, in_sems.at[sem])
            copy.start()
            return copy

        table_copy = pltpu.make_async_copy(forward_ref, taps, in_sems.at[groups * tiles])
        table_copy.start()
        waiting = {}
        if mirror is None:
            out_ref, ahead_ref = refs[:-3]
            for i in range(groups * tiles):
                waiting[i] = fetch(i, 1 - core, held.at[i], i)
            late = [
                fetch(i, core, ahead_ref.at[i], groups * tiles + 1 + i) for i in range(AHEAD)
            ]
            slots = range(groups)
        else:
            mirror_ref, ahead_ref, out_ref, table_ref = refs[:-3]
            for i in range(AHEAD, groups * tiles):
                waiting[i] = fetch(i, core, held.at[i], i)
            late = []
            deal(mirror_ref, table_ref)
            slots = [table_ref[OWN_SLOT + g] for g in range(groups)]
        table_copy.wait()
        two = two_shots(taps)
        for i in range(groups * tiles):
            g, s = divmod(i, tiles)
            if i in waiting:
                waiting[i].wait()
            block_ref = held if i in waiting else ahead_ref
            found = []
            for q in range(0, SUBLANES, 2):
                both = jnp.concatenate([block_ref[i, q], block_ref[i, q + 1]], axis=1)
                found.append(
                    lax.dot_general(
                        two, both, (((1,), (1,)), ((), ())), preferred_element_type=jnp.float32
                    )
                )
            found = jnp.concatenate(found, axis=0).reshape((SUBLANES, parts, width))
            found = jnp.transpose(found, (1, 0, 2)).reshape((parts // 2, 2, SUBLANES, width))
            window = slice(s * SUBLANES, (s + 1) * SUBLANES)
            out_ref[:, slots[g], :, window, :] = found.astype(jnp.bfloat16)
        for copy in late:
            copy.wait()

    scratch = [
        pltpu.VMEM((groups * tiles, SUBLANES, width, time), jnp.bfloat16),
        pltpu.VMEM((parts, time), jnp.bfloat16),
        pltpu.SemaphoreType.DMA((groups * tiles + 1 + AHEAD,)),
    ]
    if mirror is None:
        return pl.pallas_call(
            body,
            in_specs=[HBM, HBM],
            out_specs=[VMEM, VMEM],
            out_shape=[on_chip(shape), on_chip(early)],
            scratch_shapes=scratch,
            compiler_params=params(16),
            name="forward",
        )(forward, records)
    return pl.pallas_call(
        body,
        in_specs=[HBM, HBM, SMEM, VMEM],
        out_specs=[VMEM, SMEM],
        out_shape=[on_chip(shape), jax.ShapeDtypeStruct((ENTRIES,), jnp.int32)],
        scratch_shapes=scratch,
        compiler_params=params(16),
        name="forward",
    )(forward, records, mirror, ahead)


def multiply(j, slot, scale_ref, spectra_ref, own_ref, other_ref):
    size, recv = spectra_ref.shape[-2:]
    blocks, _, _, shots, width = other_ref.shape
    step = ROWS // shots
    core = lax.axis_index("core")
    scale = -scale_ref[...] / math.sqrt(2.0 * recv)

    def dot(a, b):
        return jnp.dot(a, b, preferred_element_type=jnp.float32)

    def scaled(part):
        return (part * scale).astype(jnp.bfloat16)

    def times(left_re, left_im):
        both = left_re + left_im
        first = dot(left_re, spectra_ref[1 - j, 0])
        second = dot(left_im, spectra_ref[1 - j, 1])
        third = dot(both, spectra_ref[1 - j, 2])
        return first - second, third - first - second

    for m in range(blocks // step):
        window = pl.ds(m * ROWS, ROWS)
        real_1, imag_1 = times(
            scaled(spectra_ref[j, 0, window, :].astype(jnp.float32)),
            scaled(spectra_ref[j, 1, window, :].astype(jnp.float32)),
        )
        real_2, imag_2 = times(scaled(real_1), scaled(imag_1))
        for c, total in enumerate((real_1 + real_2, imag_1 + imag_2)):
            total = total.astype(jnp.bfloat16)
            low = total[:, :width].reshape((step, shots, width))
            high = total[:, width:].reshape((step, shots, width))
            own_ref[pl.ds(m * step, step), slot, c] = jnp.where(core == 0, low, high)
            other_ref[pl.ds(m * step, step), j, c] = jnp.where(core == 0, high, low)


def chain(table, surface, kept, got):
    blocks, _, parts, shots, width = kept.shape
    size = blocks * shots

    def body(table_ref, scale_ref, kept_ref, got_ref, own_ref, other_ref, spectra_ref):
        core = lax.axis_index("core")
        slots = [table_ref[OWN_MEMBER + j] for j in range(2)]
        for value in range(2):

            @pl.when(core == value)
            def _():
                here = slice(value * width, (value + 1) * width)
                there = slice((1 - value) * width, (2 - value) * width)
                for j in range(2):
                    for c in range(2):
                        spectra_ref[j, c, :, here] = kept_ref[:, slots[j], c].reshape((size, width))
                        spectra_ref[j, c, :, there] = got_ref[:, j, c].reshape((size, width))

        for j in range(2):
            spectra_ref[j, 2] = spectra_ref[j, 0] + spectra_ref[j, 1]
        for j in range(2):
            multiply(j, slots[j], scale_ref, spectra_ref, own_ref, other_ref)

    return pl.pallas_call(
        body,
        in_specs=[SMEM, VMEM, VMEM, VMEM],
        out_specs=[VMEM, VMEM],
        out_shape=[on_chip(kept.shape), on_chip(got.shape)],
        scratch_shapes=[pltpu.VMEM((2, 3, size, 2 * width), jnp.bfloat16)],
        compiler_params=params(30),
        name="chain",
    )(table, surface, kept, got)


def inverse_transform(table, inverse, total, groups, whole=None):
    _, _, parts, shots, width = total.shape
    rows, time = inverse.shape
    tiles = shots // SUBLANES
    count = len(groups)

    def body(table_ref, inverse_ref, total_ref, *refs):
        out_ref, predicted, out_sems = refs[-3:]
        core = lax.axis_index("core")
        half = core if whole is None else 1 - core
        start = pl.multiple_of(half * width, width)
        two = two_shots(inverse_ref)
        copies = []
        for i in range(count * tiles):
            n, s = divmod(i, tiles)
            g = groups[n]
            slot = table_ref[OWN_SLOT + g] if whole is None else n
            block = total_ref[:, slot, :, s * SUBLANES : (s + 1) * SUBLANES, :]
            block = block.astype(jnp.float32).reshape((rows, SUBLANES, width))
            block = jnp.transpose(block, (1, 0, 2)).astype(jnp.bfloat16)
            for q in range(0, SUBLANES, 2):
                both = jnp.concatenate([block[q], block[q + 1]], axis=0)
                traces = lax.dot_general(
                    both, two, (((0,), (0,)), ((), ())), preferred_element_type=jnp.float32
                ).astype(jnp.bfloat16)
                predicted[i, q] = traces[:, :time]
                predicted[i, q + 1] = traces[:, time:]
            target = out_ref.at[g, pl.ds(s * SUBLANES, SUBLANES), pl.ds(start, width)]
            copies.append(pltpu.make_async_copy(predicted.at[i], target, out_sems.at[i]))
            copies[-1].start()
        for copy in copies:
            copy.wait()

    specs = [SMEM, VMEM, VMEM]
    operands = [table, inverse, total]
    aliases = {}
    if whole is not None:
        specs.append(ANY)
        operands.append(whole)
        aliases = {3: 0}
    return pl.pallas_call(
        body,
        in_specs=specs,
        out_specs=ANY,
        out_shape=jax.ShapeDtypeStruct((2, shots, 2 * width, time), jnp.bfloat16),
        scratch_shapes=[
            pltpu.VMEM((count * tiles, SUBLANES, width, time), jnp.bfloat16),
            pltpu.SemaphoreType.DMA((count * tiles,)),
        ],
        input_output_aliases=aliases,
        compiler_params=params(16),
        name="inverse",
    )(*operands)


def stay(part):
    return pltpu.with_memory_space_constraint(part, pltpu.VMEM)


def other_core(part):
    return stay(lax.ppermute(part, "core", [(0, 1), (1, 0)]))


def exchange(chunks):
    blocks, count, parts, shots, width = chunks.shape
    chunks = chunks.reshape((2 * blocks, count // 2, parts, shots, width))
    chunks = lax.all_to_all(chunks, COLUMN, 0, 0, tiled=True)
    return stay(chunks.reshape((blocks, count, parts, shots, width)))


def local(records, surface, mirror):
    freqs = lax.axis_size("x") * lax.axis_size("y") * lax.axis_size("zh")
    forward, inverse = make_tables(freqs, records.shape[-1])
    forward = pltpu.with_memory_space_constraint(forward, pltpu.HBM)
    records = pltpu.with_memory_space_constraint(records, pltpu.HBM)
    sent, ahead = forward_transform(forward, records)
    chunks, table = forward_transform(forward, records, mirror, ahead)
    chunks = scatter(table, [other_core(sent)], chunks, OTHER_SLOT)
    chunks = exchange(chunks)
    got = other_core(gather(table, chunks, [OTHER_MEMBER, OTHER_MEMBER + 1]))
    own, other = chain(table, surface, chunks, got)
    chunks = scatter(table, [other_core(other)], own, OTHER_MEMBER)
    chunks = exchange(chunks)
    got = other_core(gather(table, chunks, [OTHER_SLOT, OTHER_SLOT + 1]))
    predicted = inverse_transform(table, inverse, chunks, [0, 1])
    return inverse_transform(table, inverse, got, [0, 1], predicted)


def solution(mesh):
    devices = mesh.devices.reshape((2, 2, 4, 4, 2))
    whole = Mesh(devices, ("zl", "core", "x", "y", "zh"))
    pair, shot = ("zl", "core"), ("x", "y", "zh")
    return jax.shard_map(
        local,
        mesh=whole,
        in_specs=(P(pair, shot, None, None), P(shot, None), P()),
        out_specs=P(pair, shot, None, None),
        check_vma=False,
    )
```

```python
import math

import jax
import jax.numpy as jnp
import numpy as np
from jax import lax
from jax.experimental import pallas as pl
from jax.experimental.pallas import tpu as pltpu
from jax.sharding import Mesh
from jax.sharding import PartitionSpec as P

COLUMN = ("x", "y", "zh", "zl")
ROWS = 384
SUBLANES = 8
AHEAD = 2
GROUPS = 8


def make_tables(freqs, time):
    product = np.arange(1, freqs + 1)[:, None] * np.arange(time)[None, :] % time
    phase = product * (2.0 * math.pi / time)
    parts = np.stack([np.cos(phase), -np.sin(phase)], axis=1).reshape((2 * freqs, time))
    forward = (parts * math.sqrt(2.0 / time)).astype(np.float32)
    inverse = (parts / math.sqrt(freqs)).astype(np.float32)
    return (forward.astype(jnp.bfloat16), inverse.astype(jnp.bfloat16))


OWN_SLOT = 0
OTHER_SLOT = 2
OWN_MEMBER = 4
OTHER_MEMBER = 6
ENTRIES = 8


def deal(mirror_ref, table_ref):
    half = GROUPS // 2
    chip, core = lax.axis_index("zl"), lax.axis_index("core")
    mirror = [mirror_ref[g] for g in range(GROUPS)]
    zero, one = jnp.int32(0), jnp.int32(1)

    def flag(condition):
        return jnp.where(condition, one, zero)

    upper = [flag(m >= half) for m in mirror]
    within = [upper[g] if g >= half else 1 - upper[g] for g in range(GROUPS)]
    crossing = GROUPS - sum(within[1:], within[0])
    low = [jnp.minimum(m, g) for g, m in enumerate(mirror)]
    color, key = [], []
    for g in range(GROUPS):
        with_first = flag(mirror[g] - half * upper[g] == 0) if g % half else one
        color.append(
            jnp.where(
                crossing == GROUPS,
                flag(low[g] >= half // 2),
                jnp.where(crossing == half, 1 - within[g], 1 - with_first),
            )
        )
        key.append(jnp.where(within[g] == 1, g, low[g]))
    place = []
    for g in range(GROUPS):
        rank = zero
        for other in range(g // half * half, g // half * half + half):
            if other != g:
                rank = rank + flag(color[g] == color[other]) * flag(key[other] < key[g])
        place.append(2 * color[g] + rank)
    mine = [jnp.where(chip == 0, place[g], place[half + g]) for g in range(half)]
    for g in range(2):
        table_ref[OWN_SLOT + g] = jnp.where(core == 0, mine[g], mine[2 + g])
        table_ref[OTHER_SLOT + g] = jnp.where(core == 0, mine[2 + g], mine[g])
    mixed = jnp.where(chip == 0, flag(crossing == GROUPS), flag(crossing >= half))
    for j in range(2):
        table_ref[OWN_MEMBER + j] = jnp.where(mixed == 1, 2 * j + core, 2 * core + j)
        table_ref[OTHER_MEMBER + j] = jnp.where(mixed == 1, 2 * j + 1 - core, 2 * (1 - core) + j)


def params(limit):
    return pltpu.CompilerParams(vmem_limit_bytes=limit << 20)


SMEM = pl.BlockSpec(memory_space=pltpu.SMEM)
VMEM = pl.BlockSpec(memory_space=pltpu.VMEM)
ANY = pl.BlockSpec(memory_space=pl.ANY)
HBM = pl.BlockSpec(memory_space=pltpu.HBM)


def copy_all(pairs, sems):
    copies = [pltpu.make_async_copy(a, b, sems.at[i]) for i, (a, b) in enumerate(pairs)]
    for copy in copies:
        copy.start()
    for copy in copies:
        copy.wait()


def gather(table, whole, entries):
    blocks, _, parts, shots, width = whole.shape
    count = len(entries)

    def body(table_ref, whole_ref, part_ref, sems):
        copy_all(
            [(whole_ref.at[:, table_ref[e]], part_ref.at[:, j]) for j, e in enumerate(entries)],
            sems,
        )

    return pl.pallas_call(
        body,
        in_specs=[SMEM, VMEM],
        out_specs=VMEM,
        out_shape=on_chip((blocks, count, parts, shots, width)),
        scratch_shapes=[pltpu.SemaphoreType.DMA((count,))],
        compiler_params=params(8),
        name="gather",
    )(table, whole)


def scatter(table, parts, whole, slots):
    places = [(p, j) for p, part in enumerate(parts) for j in range(part.shape[1])]

    def body(table_ref, *refs):
        out_ref, sems = refs[-2:]
        copy_all(
            [
                (refs[p].at[:, j], out_ref.at[:, table_ref[slots + i]])
                for i, (p, j) in enumerate(places)
            ],
            sems,
        )

    return pl.pallas_call(
        body,
        in_specs=[SMEM] + [VMEM] * (len(parts) + 1),
        out_specs=VMEM,
        out_shape=on_chip(whole.shape),
        scratch_shapes=[pltpu.SemaphoreType.DMA((len(places),))],
        input_output_aliases={len(parts) + 1: 0},
        compiler_params=params(8),
        name="scatter",
    )(table, *parts, whole)


def on_chip(shape):
    return pltpu.VMEM(shape, jnp.bfloat16)


def two_shots(taps_ref):
    taps = taps_ref[...]
    blank = jnp.zeros_like(taps)
    return jnp.concatenate(
        [jnp.concatenate([taps, blank], axis=1), jnp.concatenate([blank, taps], axis=1)], axis=0
    )


def forward_transform(forward, records, mirror=None, ahead=None):
    groups, shots, recv, time = records.shape
    parts = forward.shape[0]
    width = recv // 2
    tiles = shots // SUBLANES
    count = groups if mirror is None else 2 * groups
    shape = (parts // 2, count, 2, shots, width)
    early = (AHEAD, SUBLANES, width, time)

    def body(forward_ref, records_ref, *refs):
        held, taps, in_sems = refs[-3:]
        core = lax.axis_index("core")

        def fetch(i, half, target, sem):
            g, s = divmod(i, tiles)
            start = pl.multiple_of(half * width, width)
            source = records_ref.at[g, pl.ds(s * SUBLANES, SUBLANES), pl.ds(start, width)]
            copy = pltpu.make_async_copy(source, target, in_sems.at[sem])
            copy.start()
            return copy

        table_copy = pltpu.make_async_copy(forward_ref, taps, in_sems.at[groups * tiles])
        table_copy.start()
        waiting = {}
        if mirror is None:
            out_ref, ahead_ref = refs[:-3]
            for i in range(groups * tiles):
                waiting[i] = fetch(i, 1 - core, held.at[i], i)
            late = [
                fetch(i, core, ahead_ref.at[i], groups * tiles + 1 + i) for i in range(AHEAD)
            ]
            slots = range(groups)
        else:
            mirror_ref, ahead_ref, out_ref, table_ref = refs[:-3]
            for i in range(AHEAD, groups * tiles):
                waiting[i] = fetch(i, core, held.at[i], i)
            late = []
            deal(mirror_ref, table_ref)
            slots = [table_ref[OWN_SLOT + g] for g in range(groups)]
        table_copy.wait()
        two = two_shots(taps)
        for i in range(groups * tiles):
            g, s = divmod(i, tiles)
            if i in waiting:
                waiting[i].wait()
            block_ref = held if i in waiting else ahead_ref
            found = []
            for q in range(0, SUBLANES, 2):
                both = jnp.concatenate([block_ref[i, q], block_ref[i, q + 1]], axis=1)
                found.append(
                    lax.dot_general(
                        two, both, (((1,), (1,)), ((), ())), preferred_element_type=jnp.float32
                    )
                )
            found = jnp.concatenate(found, axis=0).reshape((SUBLANES, parts, width))
            found = jnp.transpose(found, (1, 0, 2)).reshape((parts // 2, 2, SUBLANES, width))
            window = slice(s * SUBLANES, (s + 1) * SUBLANES)
            out_ref[:, slots[g], :, window, :] = found.astype(jnp.bfloat16)
        for copy in late:
            copy.wait()

    scratch = [
        pltpu.VMEM((groups * tiles, SUBLANES, width, time), jnp.bfloat16),
        pltpu.VMEM((parts, time), jnp.bfloat16),
        pltpu.SemaphoreType.DMA((groups * tiles + 1 + AHEAD,)),
    ]
    if mirror is None:
        return pl.pallas_call(
            body,
            in_specs=[HBM, HBM],
            out_specs=[VMEM, VMEM],
            out_shape=[on_chip(shape), on_chip(early)],
            scratch_shapes=scratch,
            compiler_params=params(16),
            name="forward",
        )(forward, records)
    return pl.pallas_call(
        body,
        in_specs=[HBM, HBM, SMEM, VMEM],
        out_specs=[VMEM, SMEM],
        out_shape=[on_chip(shape), jax.ShapeDtypeStruct((ENTRIES,), jnp.int32)],
        scratch_shapes=scratch,
        compiler_params=params(16),
        name="forward",
    )(forward, records, mirror, ahead)


def multiply(j, slot, scale_ref, spectra_ref, own_ref, other_ref):
    size, recv = spectra_ref.shape[-2:]
    blocks, _, _, shots, width = other_ref.shape
    step = ROWS // shots
    core = lax.axis_index("core")
    scale = -scale_ref[...] / math.sqrt(2.0 * recv)

    def dot(a, b):
        return jnp.dot(a, b, preferred_element_type=jnp.float32)

    def scaled(part):
        return (part * scale).astype(jnp.bfloat16)

    def times(left_re, left_im):
        both = left_re + left_im
        first = dot(left_re, spectra_ref[1 - j, 0])
        second = dot(left_im, spectra_ref[1 - j, 1])
        third = dot(both, spectra_ref[1 - j, 2])
        return first - second, third - first - second

    for m in range(blocks // step):
        window = pl.ds(m * ROWS, ROWS)
        real_1, imag_1 = times(
            scaled(spectra_ref[j, 0, window, :].astype(jnp.float32)),
            scaled(spectra_ref[j, 1, window, :].astype(jnp.float32)),
        )
        real_2, imag_2 = times(scaled(real_1), scaled(imag_1))
        for c, total in enumerate((real_1 + real_2, imag_1 + imag_2)):
            total = total.astype(jnp.bfloat16)
            low = total[:, :width].reshape((step, shots, width))
            high = total[:, width:].reshape((step, shots, width))
            own_ref[pl.ds(m * step, step), slot, c] = jnp.where(core == 0, low, high)
            other_ref[pl.ds(m * step, step), j, c] = jnp.where(core == 0, high, low)


def chain(table, surface, kept, got):
    blocks, _, parts, shots, width = kept.shape
    size = blocks * shots

    def body(table_ref, scale_ref, kept_ref, got_ref, own_ref, other_ref, spectra_ref):
        core = lax.axis_index("core")
        slots = [table_ref[OWN_MEMBER + j] for j in range(2)]
        def assemble(j):
            for c in range(2):
                kept = kept_ref[:, slots[j], c].reshape((size, width))
                got = got_ref[:, j, c].reshape((size, width))
                spectra_ref[j, c, :, :width] = jnp.where(core == 0, kept, got)
                spectra_ref[j, c, :, width:] = jnp.where(core == 0, got, kept)

        assemble(1)
        assemble(0)
        spectra_ref[1, 2] = spectra_ref[1, 0] + spectra_ref[1, 1]
        multiply(0, slots[0], scale_ref, spectra_ref, own_ref, other_ref)
        spectra_ref[0, 2] = spectra_ref[0, 0] + spectra_ref[0, 1]
        multiply(1, slots[1], scale_ref, spectra_ref, own_ref, other_ref)

    return pl.pallas_call(
        body,
        in_specs=[SMEM, VMEM, VMEM, VMEM],
        out_specs=[VMEM, VMEM],
        out_shape=[on_chip(kept.shape), on_chip(got.shape)],
        scratch_shapes=[pltpu.VMEM((2, 3, size, 2 * width), jnp.bfloat16)],
        compiler_params=params(30),
        name="chain",
    )(table, surface, kept, got)


def inverse_transform(table, inverse, total, groups, whole=None):
    _, _, parts, shots, width = total.shape
    rows, time = inverse.shape
    tiles = shots // SUBLANES
    count = len(groups)

    def body(table_ref, inverse_ref, total_ref, *refs):
        out_ref, predicted, out_sems = refs[-3:]
        core = lax.axis_index("core")
        half = core if whole is None else 1 - core
        start = pl.multiple_of(half * width, width)
        two = two_shots(inverse_ref)
        copies = []
        for i in range(count * tiles):
            n, s = divmod(i, tiles)
            g = groups[n]
            slot = table_ref[OWN_SLOT + g] if whole is None else n
            block = total_ref[:, slot, :, s * SUBLANES : (s + 1) * SUBLANES, :]
            block = block.astype(jnp.float32).reshape((rows, SUBLANES, width))
            block = jnp.transpose(block, (1, 0, 2)).astype(jnp.bfloat16)
            for q in range(0, SUBLANES, 2):
                both = jnp.concatenate([block[q], block[q + 1]], axis=0)
                traces = lax.dot_general(
                    both, two, (((0,), (0,)), ((), ())), preferred_element_type=jnp.float32
                ).astype(jnp.bfloat16)
                predicted[i, q] = traces[:, :time]
                predicted[i, q + 1] = traces[:, time:]
                if q % 4 == 2:
                    source = predicted.at[i, pl.ds(q - 2, 4)]
                    target = out_ref.at[g, pl.ds(s * SUBLANES + q - 2, 4), pl.ds(start, width)]
                    sem = out_sems.at[len(copies)]
                    copies.append(pltpu.make_async_copy(source, target, sem))
                    copies[-1].start()
        for copy in copies:
            copy.wait()

    specs = [SMEM, VMEM, VMEM]
    operands = [table, inverse, total]
    aliases = {}
    if whole is not None:
        specs.append(ANY)
        operands.append(whole)
        aliases = {3: 0}
    return pl.pallas_call(
        body,
        in_specs=specs,
        out_specs=ANY,
        out_shape=jax.ShapeDtypeStruct((2, shots, 2 * width, time), jnp.bfloat16),
        scratch_shapes=[
            pltpu.VMEM((count * tiles, SUBLANES, width, time), jnp.bfloat16),
            pltpu.SemaphoreType.DMA((2 * count * tiles,)),
        ],
        input_output_aliases=aliases,
        compiler_params=params(16),
        name="inverse",
    )(*operands)


def stay(part):
    return pltpu.with_memory_space_constraint(part, pltpu.VMEM)


def other_core(part):
    return stay(lax.ppermute(part, "core", [(0, 1), (1, 0)]))


def exchange(chunks):
    blocks, count, parts, shots, width = chunks.shape
    chunks = chunks.reshape((2 * blocks, count // 2, parts, shots, width))
    chunks = lax.all_to_all(chunks, COLUMN, 0, 0, tiled=True)
    return stay(chunks.reshape((blocks, count, parts, shots, width)))


def local(records, surface, mirror):
    freqs = lax.axis_size("x") * lax.axis_size("y") * lax.axis_size("zh")
    forward, inverse = make_tables(freqs, records.shape[-1])
    forward = pltpu.with_memory_space_constraint(forward, pltpu.HBM)
    records = pltpu.with_memory_space_constraint(records, pltpu.HBM)
    sent, ahead = forward_transform(forward, records)
    chunks, table = forward_transform(forward, records, mirror, ahead)
    chunks = scatter(table, [other_core(sent)], chunks, OTHER_SLOT)
    chunks = exchange(chunks)
    got = other_core(gather(table, chunks, [OTHER_MEMBER, OTHER_MEMBER + 1]))
    own, other = chain(table, surface, chunks, got)
    chunks = scatter(table, [other_core(other)], own, OTHER_MEMBER)
    chunks = exchange(chunks)
    got = other_core(gather(table, chunks, [OTHER_SLOT, OTHER_SLOT + 1]))
    predicted = inverse_transform(table, inverse, chunks, [0, 1])
    return inverse_transform(table, inverse, got, [0, 1], predicted)


def solution(mesh):
    devices = mesh.devices.reshape((2, 2, 4, 4, 2))
    whole = Mesh(devices, ("zl", "core", "x", "y", "zh"))
    pair, shot = ("zl", "core"), ("x", "y", "zh")
    return jax.shard_map(
        local,
        mesh=whole,
        in_specs=(P(pair, shot, None, None), P(shot, None), P()),
        out_specs=P(pair, shot, None, None),
        check_vma=False,
    )
```
